32 devices in a mesh: rows: 16 (over z, y, x), grid: 2 (over core).
Axes of the slice: x: 2, y: 2, z: 4, core: 2. Of those that a mesh axis runs over, the one named last changes fastest.
Arguments:
- library: bfloat16 [8192, 4096], P('rows', 'grid'), may hold values from -6 to 6
- col_scale: float32 [4096], replicated, may hold values from 0.5 to 2
Outputs:
- updated: float32 [4096, 4096], P('rows', 'grid')
- reflectors: float32 [4096, 64], P('rows')
The draws below stay inside these ranges and needn't reach their ends.
All inputs are finite; a program needn't handle non-finite values.
Results may differ from the reference program's by a relative error of at most 0.0003.
Values may be sent and summed in bfloat16 or wider, within the bound.
A program may use at most 128 MiB of HBM per device.

```python
import math
import jax
import jax.numpy as jnp
from jax import lax

COLS = 4096
PANEL = 64
TOTAL_ROWS = 8192


def strengthened(entries, key, source, target, parts, factor):
    owner, partner = [(jnp.arange(entries.shape[dim]) // (entries.shape[dim] // parts)).reshape([-1 if axis == dim else 1 for axis in range(entries.ndim)]) for dim in (source, target)]
    chosen = jax.random.permutation(key, parts)[partner]
    strong = (owner == chosen) | (owner == (partner + parts // 2) % parts)
    return jnp.where(strong, factor * entries, entries)


def block_scale(key, shape, cuts, least, high):
    def one(dim, parts):
        heights = jax.random.uniform(jax.random.fold_in(jax.random.fold_in(key, 6), dim), (parts,), jnp.float32, least / len(cuts), high / len(cuts))
        return jnp.repeat(jnp.exp(heights), shape[dim] // parts).reshape((-1,) + (1,) * (len(shape) - dim - 1))

    factor_of = one(*cuts[0])
    for cut in cuts[1:]:
        factor_of = factor_of * one(*cut)
    return factor_of


def bell_draw_with(stream_key, shape, scale, most, split, heavy, held_as=jnp.bfloat16):
    drawn = scale * jax.random.normal(stream_key, shape, jnp.float32)
    if split:
        drawn = drawn * block_scale(stream_key, shape, split, -0.22, 0.18)
    return jnp.clip(strengthened(drawn, jax.random.fold_in(stream_key, 3), *heavy), -most, most).astype(held_as)


def setup_inputs(seed: int = 0) -> dict:
    arg_keys = jax.random.split(jax.random.key(seed), 3)
    return {
        "library": bell_draw_with(arg_keys[0], (TOTAL_ROWS, COLS), 1.0, 6.0, ((0, 16), (1, 2)), (0, 1, 16, 2.0)),
        "col_scale": jnp.clip(jnp.exp(jax.random.uniform(arg_keys[1], (COLS,), jnp.float32, math.log(0.5), math.log(2.0))), 0.5, 2.0),
    }


def reflect_panel(panel):
    size, width = panel.shape
    row_line = jnp.arange(size)
    col_line = jnp.arange(width)
    vectors = jnp.zeros((size, width), jnp.float32)
    factor = jnp.zeros((width, width), jnp.float32)

    def one_step(step, carry):
        work, vectors, factor = carry
        column = lax.optimization_barrier(jnp.sum(jnp.where(col_line[None, :] == step, work, 0.0), axis=1))
        column = jnp.where(row_line >= step, column, 0.0)
        pivot = jnp.sum(jnp.where(row_line == step, column, 0.0))
        length = jnp.sqrt(jnp.sum(column * column))
        sign_factor = jnp.where(pivot >= 0.0, 1.0, -1.0)
        vector = column + jnp.where(row_line == step, sign_factor * length, 0.0)
        scale = 2.0 / jnp.sum(vector * vector)
        project = jnp.dot(vector, work, precision=lax.Precision.HIGHEST)
        work = work - scale * vector[:, None] * project[None, :]
        coupling = jnp.dot(vector, vectors, precision=lax.Precision.HIGHEST)
        column_t = -scale * jnp.dot(factor, coupling, precision=lax.Precision.HIGHEST)
        column_t = column_t + jnp.where(col_line == step, scale, 0.0)
        factor = jnp.where(col_line[None, :] == step, column_t[:, None], factor)
        vectors = jnp.where(col_line[None, :] == step, vector[:, None], vectors)
        return (work, vectors, factor)
    work, vectors, factor = lax.fori_loop(0, width, one_step, (panel, vectors, factor))
    return (vectors, factor)

def reference(library, col_scale):
    total = library.shape[0]
    gram = lax.dot_general(library, library, (((0,), (0,)), ((), ())), preferred_element_type=jnp.float32)
    gram = gram * (col_scale[:, None] * col_scale[None, :] / total)
    panel = gram[:, :PANEL]
    vectors, factor = reflect_panel(panel)
    cross = jnp.dot(vectors.T, gram, precision=lax.Precision.HIGHEST)
    mixed = jnp.dot(factor.T, cross, precision=lax.Precision.HIGHEST)
    updated = gram - jnp.dot(vectors, mixed, precision=lax.Precision.HIGHEST)
    return (updated, vectors)
```

```python
import functools

import jax
import jax.numpy as jnp
from jax import lax
from jax.experimental import pallas as pl
from jax.experimental.pallas import tpu as pltpu
from jax.sharding import PartitionSpec as P

PANEL = 64
HIGH = lax.Precision.HIGHEST
MESH = pl.DeviceIdType.MESH


def reflect(vectors_ref, weights_ref, work, inner, taus):
    width, size = work.shape
    lane = lax.broadcasted_iota(jnp.int32, (1, size), 1)
    for base in range(0, width, 8):

        def one_step(step, carry, base=base):
            place = base + step
            row = work[pl.ds(place, 1), :]
            row = jnp.where(lane >= place, row, 0.0)
            pivot = jnp.sum(jnp.where(lane == place, row, 0.0), axis=1, keepdims=True)
            length = jnp.sqrt(jnp.sum(row * row, axis=1, keepdims=True))
            signed = jnp.where(pivot >= 0.0, length, -length)
            vector = row + jnp.where(lane == place, signed, 0.0)
            tau = 1.0 / (length * (length + jnp.abs(pivot)))
            rest = work[base:, :]
            project = jnp.sum(rest * vector, axis=1, keepdims=True)
            work[base:, :] = rest - (tau * project) * vector
            vectors_ref[pl.ds(place, 1), :] = vector
            taus[pl.ds(place, 1), :] = jnp.broadcast_to(tau, (1, 128))
            return carry

        lax.fori_loop(0, 8, one_step, 0)
    vectors = vectors_ref[...]
    inner[...] = lax.dot_general(
        vectors, vectors, (((1,), (1,)), ((), ())), precision=HIGH, preferred_element_type=jnp.float32
    )
    across = lax.broadcasted_iota(jnp.int32, (width, width), 1)
    down = lax.broadcasted_iota(jnp.int32, (width, 1), 0)

    def factor_step(place, factor):
        tau = taus[pl.ds(place, 1), 0:1]
        coupling = jnp.where(across < place, inner[pl.ds(place, 1), :] * factor, 0.0)
        column = -tau * jnp.sum(coupling, axis=1, keepdims=True)
        column = column + jnp.where(down == place, tau, 0.0)
        return jnp.where(across == place, column, factor)

    factor = lax.fori_loop(0, width, factor_step, jnp.zeros((width, width), jnp.float32))
    weights_ref[...] = lax.dot_general(
        factor, vectors, (((0,), (0,)), ((), ())), precision=HIGH, preferred_element_type=jnp.float32
    )


def remote(source, target, send, recv, place):
    return pltpu.make_async_remote_copy(
        src_ref=source, dst_ref=target, send_sem=send, recv_sem=recv,
        device_id=place, device_id_type=pl.DeviceIdType.MESH,
    )


def sum_rows(count, part, landed, out, sems):
    me, core = lax.axis_index("rows"), lax.axis_index("grid")
    send, recv, send_back, recv_back = sems

    def scatter(step):
        peer = lax.rem(me + step, count)
        return remote(part.at[peer], landed.at[step], send.at[step], recv.at[step], (peer, core))

    def spread(step):
        peer = lax.rem(me + step, count)
        return remote(out.at[me], out.at[me], send_back.at[step], recv_back.at[step], (peer, core))

    def arrival(step):
        peer = lax.rem(me + count - step, count)
        return remote(out.at[peer], out.at[peer], send_back.at[step], recv_back.at[step], (peer, core))

    def loop(action):
        def body(step, carry):
            action(step)
            return carry
        lax.fori_loop(1, count, body, 0)

    loop(lambda step: scatter(step).start())
    loop(lambda step: scatter(step).wait_recv())
    total = part[me]
    for step in range(1, count):
        total = total + landed[step]
    out[me] = total
    loop(lambda step: spread(step).start())
    loop(lambda step: arrival(step).wait_recv())
    loop(lambda step: scatter(step).wait_send())
    loop(lambda step: spread(step).wait_send())


def panel_kernel(
    count, cores, part_ref, library_ref, scale_ref, vectors_ref, mixed_ref,
    part, landed, gathered, part_two, landed_two, gathered_two, halves,
    weights, work, inner, taus, row_sems, row_sems_two, core_sems, half_sems,
):
    me, core = lax.axis_index("rows"), lax.axis_index("grid")
    width, block = part_ref.shape
    per = width // count
    barrier = pltpu.get_barrier_semaphore()

    def greet(step, carry):
        pl.semaphore_signal(
            barrier, inc=1, device_id=(lax.rem(me + step, count), core), device_id_type=pl.DeviceIdType.MESH
        )
        return carry

    lax.fori_loop(1, count, greet, 0)
    for step in range(1, cores):
        pl.semaphore_signal(
            barrier, inc=1, device_id=(me, lax.rem(core + step, cores)), device_id_type=pl.DeviceIdType.MESH
        )
    for place in range(count):
        part[place] = part_ref[place * per:(place + 1) * per, :]
    pl.semaphore_wait(barrier, count + cores - 2)

    sum_rows(count, part, landed, gathered.at[core], [row_sems.at[k] for k in range(4)])
    shares = []
    for step in range(1, cores):
        peer = lax.rem(core + step, cores)
        shares.append(
            remote(gathered.at[core], gathered.at[core], core_sems.at[0, step], core_sems.at[1, step], (me, peer))
        )
        shares[-1].start()
    for step in range(1, cores):
        peer = lax.rem(core + cores - step, cores)
        remote(
            gathered.at[peer], gathered.at[peer], core_sems.at[0, step], core_sems.at[1, step], (me, peer)
        ).wait_recv()
    for share in shares:
        share.wait_send()
    for half in range(cores):
        for place in range(count):
            work[place * per:(place + 1) * per, half * block:(half + 1) * block] = gathered[half, place]

    reflect(vectors_ref, weights, work, inner, taus)

    step_cols = min(block, 512)
    halves[0] = jnp.zeros_like(halves[0])
    for start in range(0, block, step_cols):
        cols = slice(start, start + step_cols)
        own = weights[:, pl.ds(pl.multiple_of(core * block + start, 128), step_cols)] * scale_ref[:, cols]
        halves[0] += lax.dot_general(
            own, library_ref[:, cols].astype(jnp.float32), (((1,), (1,)), ((), ())),
            precision=HIGH, preferred_element_type=jnp.float32,
        )
    shares = []
    for step in range(1, cores):
        peer = lax.rem(core + step, cores)
        shares.append(
            remote(halves.at[0], halves.at[step], half_sems.at[0, step], half_sems.at[1, step], (me, peer))
        )
        shares[-1].start()
    for share in shares:
        share.wait()
    summed = halves[0]
    for step in range(1, cores):
        summed = summed + halves[step]
    for start in range(0, block, step_cols):
        cols = slice(start, start + step_cols)
        chunk = jnp.dot(
            summed, library_ref[:, cols].astype(jnp.float32), precision=HIGH, preferred_element_type=jnp.float32
        )
        for place in range(count):
            part_two[place, :, cols] = chunk[place * per:(place + 1) * per, :]
    sum_rows(count, part_two, landed_two, gathered_two, [row_sems_two.at[k] for k in range(4)])
    for place in range(count):
        mixed_ref[place * per:(place + 1) * per, :] = gathered_two[place] * scale_ref[...]


def panel_chain(part, library, scale, count, cores):
    width, block = part.shape
    rows_dev = library.shape[0]
    per = width // count
    size = block * cores
    real = jnp.float32
    slices = pltpu.VMEM((count, per, block), real)
    return pl.pallas_call(
        functools.partial(panel_kernel, count, cores),
        out_shape=(jax.ShapeDtypeStruct((width, size), real), jax.ShapeDtypeStruct((width, block), real)),
        in_specs=[pl.BlockSpec(memory_space=pltpu.VMEM)] * 3,
        out_specs=(pl.BlockSpec(memory_space=pltpu.VMEM),) * 2,
        scratch_shapes=[
            slices, slices, pltpu.VMEM((cores, count, per, block), real),
            slices, slices, slices, pltpu.VMEM((cores, width, rows_dev), real),
            pltpu.VMEM((width, size), real), pltpu.VMEM((width, size), real),
            pltpu.VMEM((width, width), real), pltpu.VMEM((width, 128), real),
            pltpu.SemaphoreType.DMA((4, count)), pltpu.SemaphoreType.DMA((4, count)),
            pltpu.SemaphoreType.DMA((2, cores)), pltpu.SemaphoreType.DMA((2, cores)),
        ],
        compiler_params=pltpu.CompilerParams(
            vmem_limit_bytes=32 << 20, collective_id=0, has_side_effects=True
        ),
        cost_estimate=pl.CostEstimate(flops=20_000_000_000, bytes_accessed=200_000_000, transcendentals=0),
    )(part, library, scale)


X_ITEMS = (
    ("own", 0, 0), ("own", 1, 2), ("own", 1, 0), ("fwd", 0, 0), ("own", 0, 1), ("fwd", 0, 1),
    ("own", 1, 3), ("own", 1, 1), ("fwd", 0, 2), ("own", 0, 2), ("fwd", 0, 3), ("own", 0, 3),
)
Y_ITEMS = (
    ("own", 0, 0), ("own", 0, 1), ("own", 1, 0), ("fwd", 1, 0), ("own", 1, 2), ("fwd", 1, 2),
    ("own", 0, 3), ("own", 0, 2), ("fwd", 1, 1), ("own", 1, 1), ("fwd", 1, 3), ("own", 1, 3),
)
ITEMS = {1: X_ITEMS, 2: Y_ITEMS}
STEPS = ((0, 0), (1, 0), (0, 1), (1, 2), (0, 2), (1, 1), (0, 3), (1, 3))
READY = (4, 4, 6, 6, 10, 10, 12, 12)
TOP = 2.0 ** 15.5
LEAST = 2.0 ** -125


def flip(place, mask):
    low, high = lax.rem(place, 2), place // 2
    low = 1 - low if mask & 1 else low
    high = 1 - high if mask & 2 else high
    return high * 2 + low


def encode(value, target):
    size = value.shape[0]
    peak = jnp.max(jnp.max(jnp.abs(value), axis=0, keepdims=True), axis=1, keepdims=True)
    unit = jnp.maximum(peak, 1e-30).astype(jnp.bfloat16)
    target[size:size + 16, :] = jnp.broadcast_to(unit, (16, value.shape[1]))
    level = value * (TOP / unit.astype(jnp.float32))
    square = level * level
    fourth = square * square
    eighth = fourth * fourth
    target[0:size, :] = jnp.where(level < 0.0, -eighth, eighth).astype(jnp.bfloat16)


def decode(source):
    size = source.shape[0] - 16
    unit = source[size:size + 16, :].astype(jnp.float32)[0:1, 0:1]
    code = source[0:size, :].astype(jnp.float32)
    second = lax.rsqrt(lax.rsqrt(jnp.maximum(jnp.abs(code), LEAST)))
    value = second * lax.rsqrt(second) * (unit * (1.0 / TOP))
    return jnp.where(code < 0.0, -value, value)


def gram_kernel(
    library_ref, row_scale_ref, col_scale_ref, vectors_ref, mixed_ref, updated_ref,
    whole, left, prod, code_a, code_c, land_a, land_b, land_c,
    plane_send, plane_recv, own_sem, left_send, left_recv, z_send, z_recv,
):
    me, core = lax.axis_index("rows"), lax.axis_index("grid")
    far, near = left.shape[0], 4
    place, level = lax.rem(me, near), me // near
    samples = library_ref.shape[0]
    size = left.shape[1]
    buddy = level + 1 - 2 * lax.rem(level, 2)
    base = 2 * (1 - level // 2)
    inner = lax.rem(level + 1, far) // 2 == 1
    outer = lax.rem(level + 1, far) // 2 == 0

    def chip(mask):
        return (level * near + flip(place, mask), core)

    def floor(which):
        return (which * near + place, core)

    barrier = pltpu.get_barrier_semaphore()
    for target in (chip(1), chip(2), floor(lax.rem(level + 1, far)), floor(lax.rem(level + 2, far)),
                   floor(lax.rem(level + 3, far)), (me, 1 - core)):
        pl.semaphore_signal(barrier, inc=1, device_id=target, device_id_type=MESH)
    pl.semaphore_wait(barrier, 6)

    def columns(zz, group):
        return pl.ds(pl.multiple_of((zz * near + group) * size, size), size)

    def spot(zz, r, source):
        return whole.at[zz * near + r, pl.ds(source * samples, samples)]

    def item(mask, k):
        kind, zz, r = ITEMS[mask][k]
        if kind == "own":
            source = library_ref.at[:, columns(zz, flip(place, r ^ mask))]
            target = spot(zz, r, mask)
        else:
            source = spot(zz, r ^ mask, 3 ^ mask)
            target = spot(zz, r, 3)
        return remote(source, target, plane_send.at[mask - 1, k], plane_recv.at[mask - 1, k], chip(mask))

    seen, sent = set(), []

    def arrive(mask, k):
        if (mask, k) not in seen:
            seen.add((mask, k))
            item(mask, k).wait_recv()

    def send(mask, k):
        kind, zz, r = ITEMS[mask][k]
        if kind == "fwd":
            arrive(3 ^ mask, ITEMS[3 ^ mask].index(("own", zz, r ^ mask)))
        item(mask, k).start()
        sent.append((mask, k))

    def both(action, k):
        action(1, k)
        action(2, k)

    copies = []
    for zz in range(2):
        for r in range(4):
            copies.append(pltpu.make_async_copy(
                library_ref.at[:, columns(zz, flip(place, r))], spot(zz, r, 0), own_sem.at[zz * near + r]))
    copies[0].start()
    copies[near].start()
    for k in range(3):
        both(send, k)
    for index, copy in enumerate(copies):
        if index % near:
            copy.start()

    def piece(zz, source, half):
        block = left.at[2 * half + zz, :, pl.ds(source * samples, samples)]
        index = zz * near + source
        return remote(block, block, left_send.at[index], left_recv.at[index], (me, 1 - core))

    def turn(zz, source):
        left[2 * core + zz, :, source * samples:(source + 1) * samples] = (
            whole[zz * near, source * samples:(source + 1) * samples, :].T
        )
        piece(zz, source, core).start()

    for zz in range(2):
        copies[zz * near].wait()
        turn(zz, 0)
    both(arrive, 0)
    turn(0, 1)
    turn(0, 2)
    both(arrive, 1)
    both(send, 3)
    both(arrive, 2)
    both(send, 4)
    turn(1, 1)
    turn(1, 2)
    both(arrive, 3)
    both(send, 5)
    both(send, 6)
    turn(0, 3)
    turn(1, 3)
    for index, copy in enumerate(copies):
        if index % near:
            copy.wait()
    for zz in range(2):
        for source in range(4):
            piece(zz, source, 1 - core).wait_recv()

    def share(t, kind, which=0):
        if kind == "a":
            return remote(code_a.at[t], land_a.at[t], z_send.at[t, 0], z_recv.at[t, 0], floor(buddy))
        if kind == "c":
            return remote(code_c.at[t, which], land_c.at[t, which], z_send.at[t, 1 + which],
                          z_recv.at[t, 1 + which], floor(buddy))
        return remote(code_c.at[t, which], land_b.at[t], z_send.at[t, 1 + which], z_recv.at[t, 3],
                      floor(base + which))

    def combine(t):
        for which in range(2):
            share(t, "c", which).wait_recv()
            encode(prod[t, base + which] + decode(land_c.at[t, which]), code_c.at[t, which])
            share(t, "b", which).start()

    last = 6
    for t, (zz, r) in enumerate(STEPS):
        for k in range(READY[t]):
            both(arrive, k)
        while last + 1 < min(12, READY[t] + 4):
            last += 1
            both(send, last)

        def product(target, carry, t=t, zz=zz, r=r):
            prod[t, target] = jnp.dot(left[target], whole[zz * near + r], preferred_element_type=jnp.float32)
            return carry

        lax.fori_loop(0, far, product, 0)

        @pl.when(outer)
        def _(t=t):
            for which in range(2):
                encode(prod[t, base + which], code_c.at[t, which])
                share(t, "c", which).start()

        encode(prod[t, buddy], code_a.at[t])
        share(t, "a").start()

        if t:
            @pl.when(inner)
            def _(t=t):
                combine(t - 1)

    @pl.when(inner)
    def _():
        combine(len(STEPS) - 1)

    for t, (zz, r) in enumerate(STEPS):
        share(t, "a").wait_recv()
        share(t, "b").wait_recv()
        total = prod[t, level] + decode(land_a.at[t]) + decode(land_b.at[t])
        cols = columns(zz, flip(place, r))
        total = total * (row_scale_ref[...] * col_scale_ref[:, cols])
        updated_ref[:, cols] = total - jnp.dot(
            vectors_ref[...], mixed_ref[:, cols], precision=HIGH, preferred_element_type=jnp.float32)

    for mask, k in sent:
        item(mask, k).wait_send()
    for zz in range(2):
        for source in range(4):
            piece(zz, source, core).wait_send()
    for t in range(len(STEPS)):
        share(t, "a").wait_send()
        for which in range(2):
            share(t, "c", which).wait_send()


def gram_update(library, row_scale, col_scale, vectors, mixed, far):
    samples, block = library.shape
    near, cores = 4, 2
    size = row_scale.shape[0]
    steps = block // size
    half = jnp.bfloat16
    coded = (size + 16, size)
    dma = pltpu.SemaphoreType.DMA
    vmem = pl.BlockSpec(memory_space=pltpu.VMEM)
    return pl.pallas_call(
        gram_kernel,
        out_shape=jax.ShapeDtypeStruct((size, block), jnp.float32),
        in_specs=[pl.BlockSpec(memory_space=pl.ANY)] + [vmem] * 4,
        out_specs=vmem,
        scratch_shapes=[
            pltpu.VMEM((steps, near * samples, size), half), pltpu.VMEM((far, size, near * samples), half),
            pltpu.VMEM((steps, far, size, size), jnp.float32),
            pltpu.VMEM((steps,) + coded, half), pltpu.VMEM((steps, 2) + coded, half),
            pltpu.VMEM((steps,) + coded, half), pltpu.VMEM((steps,) + coded, half),
            pltpu.VMEM((steps, 2) + coded, half),
            dma((2, 12)), dma((2, 12)), dma((8,)), dma((8,)), dma((8,)), dma((steps, 3)), dma((steps, 4)),
        ],
        compiler_params=pltpu.CompilerParams(
            vmem_limit_bytes=56 << 20, collective_id=1, has_side_effects=True
        ),
        cost_estimate=pl.CostEstimate(flops=9_000_000_000, bytes_accessed=10_000_000, transcendentals=0),
    )(library, row_scale, col_scale, vectors, mixed)


def per_device(library, col_scale):
    rows_dev, col_block = library.shape
    count_rows = lax.axis_size("rows")
    count_grid = lax.axis_size("grid")
    columns = col_block * count_grid
    row_block = columns // count_rows
    total = rows_dev * count_rows
    near = 1
    while near * near < count_rows:
        near *= 2
    far = count_rows // near
    grid_place = lax.axis_index("grid")
    rows_place = lax.axis_index("rows")
    near_groups = [[f * near + n for n in range(near)] for f in range(far)]
    far_groups = [[f * near + n for f in range(far)] for n in range(near)]
    own_scale = lax.dynamic_slice_in_dim(col_scale, grid_place * col_block, col_block)

    head = lax.all_gather(library[:, :PANEL], "grid", axis=0)[0]
    panel_part = lax.dot_general(
        head, library, (((0,), (0,)), ((), ())), preferred_element_type=jnp.float32
    )
    panel_part = panel_part * (col_scale[:PANEL, None] * own_scale[None, :] / total)
    vectors, mixed = panel_chain(panel_part, library, own_scale[None, :], count_rows, count_grid)
    mixed = mixed / total
    row_scale = lax.dynamic_slice_in_dim(col_scale, rows_place * row_block, row_block)
    own_vectors = lax.dynamic_slice_in_dim(vectors, rows_place * row_block, row_block, 1).T
    if near == 4 and far == 4 and count_grid == 2:
        updated = gram_update(
            library, row_scale[:, None], own_scale[None, :] / total, own_vectors, mixed, far
        )
        return (updated, own_vectors)

    whole = lax.all_gather(library, "rows", axis=0, tiled=True, axis_index_groups=near_groups)
    whole, vectors, mixed = lax.optimization_barrier((whole, vectors, mixed))
    place = rows_place % near
    blocks = whole.T.reshape(far // count_grid, near, row_block, near * rows_dev)
    left = lax.dynamic_index_in_dim(blocks, place, 1, keepdims=False)
    left = left.reshape(far // count_grid * row_block, near * rows_dev)
    left = lax.all_gather(left, "grid", axis=0, tiled=True)
    product = lax.dot_general(
        left, whole, (((1,), (0,)), ((), ())), preferred_element_type=jnp.float32
    )
    gram = lax.psum_scatter(
        product, "rows", scatter_dimension=0, tiled=True, axis_index_groups=far_groups
    )
    row_scale = lax.dynamic_slice_in_dim(col_scale, rows_place * row_block, row_block)

    own_vectors = lax.dynamic_slice_in_dim(vectors, rows_place * row_block, row_block, 1).T
    gram = gram * (row_scale[:, None] * own_scale[None, :] / total)
    updated = gram - jnp.dot(own_vectors, mixed, precision=HIGH)
    return (updated, own_vectors)


def solution(mesh):
    return jax.shard_map(
        per_device,
        mesh=mesh,
        in_specs=(P("rows", "grid"), P()),
        out_specs=(P("rows", "grid"), P("rows", None)),
        check_vma=False,
    )
```

```python
import functools

import jax
import jax.numpy as jnp
from jax import lax
from jax.experimental import pallas as pl
from jax.experimental.pallas import tpu as pltpu
from jax.sharding import PartitionSpec as P

PANEL = 64
HIGH = lax.Precision.HIGHEST
MESH = pl.DeviceIdType.MESH


def reflect(vectors_ref, weights_ref, work, inner, taus):
    width, size = work.shape
    lane = lax.broadcasted_iota(jnp.int32, (1, size), 1)
    for base in range(0, width, 8):

        def one_step(step, carry, base=base):
            place = base + step
            row = work[pl.ds(place, 1), :]
            row = jnp.where(lane >= place, row, 0.0)
            pivot = jnp.sum(jnp.where(lane == place, row, 0.0), axis=1, keepdims=True)
            length = jnp.sqrt(jnp.sum(row * row, axis=1, keepdims=True))
            signed = jnp.where(pivot >= 0.0, length, -length)
            vector = row + jnp.where(lane == place, signed, 0.0)
            tau = 1.0 / (length * (length + jnp.abs(pivot)))
            rest = work[base:, :]
            project = jnp.sum(rest * vector, axis=1, keepdims=True)
            work[base:, :] = rest - (tau * project) * vector
            vectors_ref[pl.ds(place, 1), :] = vector
            taus[pl.ds(place, 1), :] = jnp.broadcast_to(tau, (1, 128))
            return carry

        lax.fori_loop(0, 8, one_step, 0)
    vectors = vectors_ref[...]
    inner[...] = lax.dot_general(
        vectors, vectors, (((1,), (1,)), ((), ())), precision=HIGH, preferred_element_type=jnp.float32
    )
    across = lax.broadcasted_iota(jnp.int32, (width, width), 1)
    down = lax.broadcasted_iota(jnp.int32, (width, 1), 0)

    def factor_step(place, factor):
        tau = taus[pl.ds(place, 1), 0:1]
        coupling = jnp.where(across < place, inner[pl.ds(place, 1), :] * factor, 0.0)
        column = -tau * jnp.sum(coupling, axis=1, keepdims=True)
        column = column + jnp.where(down == place, tau, 0.0)
        return jnp.where(across == place, column, factor)

    factor = lax.fori_loop(0, width, factor_step, jnp.zeros((width, width), jnp.float32))
    weights_ref[...] = lax.dot_general(
        factor, vectors, (((0,), (0,)), ((), ())), precision=HIGH, preferred_element_type=jnp.float32
    )


def remote(source, target, send, recv, place):
    return pltpu.make_async_remote_copy(
        src_ref=source, dst_ref=target, send_sem=send, recv_sem=recv,
        device_id=place, device_id_type=pl.DeviceIdType.MESH,
    )


def sum_rows(count, part, landed, out, sems):
    me, core = lax.axis_index("rows"), lax.axis_index("grid")
    send, recv, send_back, recv_back = sems

    def scatter(step):
        peer = lax.rem(me + step, count)
        return remote(part.at[peer], landed.at[step], send.at[step], recv.at[step], (peer, core))

    def spread(step):
        peer = lax.rem(me + step, count)
        return remote(out.at[me], out.at[me], send_back.at[step], recv_back.at[step], (peer, core))

    def arrival(step):
        peer = lax.rem(me + count - step, count)
        return remote(out.at[peer], out.at[peer], send_back.at[step], recv_back.at[step], (peer, core))

    def loop(action):
        def body(step, carry):
            action(step)
            return carry
        lax.fori_loop(1, count, body, 0)

    loop(lambda step: scatter(step).start())
    loop(lambda step: scatter(step).wait_recv())
    total = part[me]
    for step in range(1, count):
        total = total + landed[step]
    out[me] = total
    loop(lambda step: spread(step).start())
    loop(lambda step: arrival(step).wait_recv())
    loop(lambda step: scatter(step).wait_send())
    loop(lambda step: spread(step).wait_send())


def panel_kernel(
    count, cores, part_ref, library_ref, scale_ref, vectors_ref, mixed_ref,
    part, landed, gathered, part_two, landed_two, gathered_two, halves,
    weights, work, inner, taus, row_sems, row_sems_two, core_sems, half_sems,
):
    me, core = lax.axis_index("rows"), lax.axis_index("grid")
    width, block = part_ref.shape
    per = width // count
    barrier = pltpu.get_barrier_semaphore()

    def greet(step, carry):
        pl.semaphore_signal(
            barrier, inc=1, device_id=(lax.rem(me + step, count), core), device_id_type=pl.DeviceIdType.MESH
        )
        return carry

    lax.fori_loop(1, count, greet, 0)
    for step in range(1, cores):
        pl.semaphore_signal(
            barrier, inc=1, device_id=(me, lax.rem(core + step, cores)), device_id_type=pl.DeviceIdType.MESH
        )
    for place in range(count):
        part[place] = part_ref[place * per:(place + 1) * per, :]
    pl.semaphore_wait(barrier, count + cores - 2)

    sum_rows(count, part, landed, gathered.at[core], [row_sems.at[k] for k in range(4)])
    shares = []
    for step in range(1, cores):
        peer = lax.rem(core + step, cores)
        shares.append(
            remote(gathered.at[core], gathered.at[core], core_sems.at[0, step], core_sems.at[1, step], (me, peer))
        )
        shares[-1].start()
    for step in range(1, cores):
        peer = lax.rem(core + cores - step, cores)
        remote(
            gathered.at[peer], gathered.at[peer], core_sems.at[0, step], core_sems.at[1, step], (me, peer)
        ).wait_recv()
    for share in shares:
        share.wait_send()
    for half in range(cores):
        for place in range(count):
            work[place * per:(place + 1) * per, half * block:(half + 1) * block] = gathered[half, place]

    reflect(vectors_ref, weights, work, inner, taus)

    step_cols = min(block, 512)
    halves[0] = jnp.zeros_like(halves[0])
    for start in range(0, block, step_cols):
        cols = slice(start, start + step_cols)
        own = weights[:, pl.ds(pl.multiple_of(core * block + start, 128), step_cols)] * scale_ref[:, cols]
        halves[0] += lax.dot_general(
            own, library_ref[:, cols].astype(jnp.float32), (((1,), (1,)), ((), ())),
            precision=HIGH, preferred_element_type=jnp.float32,
        )
    shares = []
    for step in range(1, cores):
        peer = lax.rem(core + step, cores)
        shares.append(
            remote(halves.at[0], halves.at[step], half_sems.at[0, step], half_sems.at[1, step], (me, peer))
        )
        shares[-1].start()
    for share in shares:
        share.wait()
    summed = halves[0]
    for step in range(1, cores):
        summed = summed + halves[step]
    for start in range(0, block, step_cols):
        cols = slice(start, start + step_cols)
        chunk = jnp.dot(
            summed, library_ref[:, cols].astype(jnp.float32), precision=HIGH, preferred_element_type=jnp.float32
        )
        for place in range(count):
            part_two[place, :, cols] = chunk[place * per:(place + 1) * per, :]
    sum_rows(count, part_two, landed_two, gathered_two, [row_sems_two.at[k] for k in range(4)])
    for place in range(count):
        mixed_ref[place * per:(place + 1) * per, :] = gathered_two[place] * scale_ref[...]


def panel_chain(part, library, scale, count, cores):
    width, block = part.shape
    rows_dev = library.shape[0]
    per = width // count
    size = block * cores
    real = jnp.float32
    slices = pltpu.VMEM((count, per, block), real)
    return pl.pallas_call(
        functools.partial(panel_kernel, count, cores),
        out_shape=(jax.ShapeDtypeStruct((width, size), real), jax.ShapeDtypeStruct((width, block), real)),
        in_specs=[pl.BlockSpec(memory_space=pltpu.VMEM)] * 3,
        out_specs=(pl.BlockSpec(memory_space=pltpu.VMEM),) * 2,
        scratch_shapes=[
            slices, slices, pltpu.VMEM((cores, count, per, block), real),
            slices, slices, slices, pltpu.VMEM((cores, width, rows_dev), real),
            pltpu.VMEM((width, size), real), pltpu.VMEM((width, size), real),
            pltpu.VMEM((width, width), real), pltpu.VMEM((width, 128), real),
            pltpu.SemaphoreType.DMA((4, count)), pltpu.SemaphoreType.DMA((4, count)),
            pltpu.SemaphoreType.DMA((2, cores)), pltpu.SemaphoreType.DMA((2, cores)),
        ],
        compiler_params=pltpu.CompilerParams(
            vmem_limit_bytes=32 << 20, collective_id=0, has_side_effects=True
        ),
        cost_estimate=pl.CostEstimate(flops=20_000_000_000, bytes_accessed=200_000_000, transcendentals=0),
    )(part, library, scale)


X_ITEMS = (
    ("own", 0, 0), ("own", 1, 2), ("own", 1, 0), ("fwd", 0, 0), ("own", 0, 1), ("fwd", 0, 1),
    ("own", 1, 3), ("own", 1, 1), ("fwd", 0, 2), ("own", 0, 2), ("fwd", 0, 3), ("own", 0, 3),
)
Y_ITEMS = (
    ("own", 0, 0), ("own", 0, 1), ("own", 1, 0), ("fwd", 1, 0), ("own", 1, 2), ("fwd", 1, 2),
    ("own", 0, 3), ("own", 0, 2), ("fwd", 1, 1), ("own", 1, 1), ("fwd", 1, 3), ("own", 1, 3),
)
ITEMS = {1: X_ITEMS, 2: Y_ITEMS}
STEPS = ((0, 0), (1, 0), (0, 1), (1, 2), (0, 2), (1, 1), (0, 3), (1, 3))
READY = (4, 4, 6, 6, 10, 10, 12, 12)
TOP = 2.0 ** 15.5
LEAST = 2.0 ** -125


def flip(place, mask):
    low, high = lax.rem(place, 2), place // 2
    low = 1 - low if mask & 1 else low
    high = 1 - high if mask & 2 else high
    return high * 2 + low


def encode(value, target):
    size = value.shape[0]
    peak = jnp.max(jnp.max(jnp.abs(value), axis=0, keepdims=True), axis=1, keepdims=True)
    unit = jnp.maximum(peak, 1e-30).astype(jnp.bfloat16)
    target[size:size + 16, :] = jnp.broadcast_to(unit, (16, value.shape[1]))
    level = value * (TOP / unit.astype(jnp.float32))
    square = level * level
    fourth = square * square
    eighth = fourth * fourth
    target[0:size, :] = jnp.where(level < 0.0, -eighth, eighth).astype(jnp.bfloat16)


def decode(source):
    size = source.shape[0] - 16
    unit = source[size:size + 16, :].astype(jnp.float32)[0:1, 0:1]
    code = source[0:size, :].astype(jnp.float32)
    second = lax.rsqrt(lax.rsqrt(jnp.maximum(jnp.abs(code), LEAST)))
    value = second * lax.rsqrt(second) * (unit * (1.0 / TOP))
    return jnp.where(code < 0.0, -value, value)


def reflect_group(base, work, vectors, taus, inner):
    width, size = work.shape
    lane = lax.broadcasted_iota(jnp.int32, (1, 128), 1)

    def one_step(step, carry):
        place = base + step
        row = work[pl.ds(place, 1), :]
        head, tail = jnp.where(lane >= place, row[:, 0:128], 0.0), row[:, 128:size]
        near = work[base:base + 8, 0:128]
        rest = work[base:base + 8, 128:size]
        square = jnp.sum(head * head, axis=1, keepdims=True) + jnp.sum(tail * tail, axis=1, keepdims=True)
        pivot = jnp.sum(jnp.where(lane == place, head, 0.0), axis=1, keepdims=True)
        project = jnp.sum(near * head, axis=1, keepdims=True) + jnp.sum(rest * tail, axis=1, keepdims=True)
        across = jnp.sum(jnp.where(lane == place, near, 0.0), axis=1, keepdims=True)
        length = jnp.sqrt(square)
        signed = jnp.where(pivot >= 0.0, length, -length)
        tau = 1.0 / (length * (length + jnp.abs(pivot)))
        weight = tau * (project + signed * across)
        head = head + jnp.where(lane == place, signed, 0.0)
        work[base:base + 8, 0:128] = near - weight * head
        work[base:base + 8, 128:size] = rest - weight * tail
        vectors[pl.ds(place, 1), :] = jnp.concatenate([head, tail], axis=1)
        taus[pl.ds(place, 1), :] = jnp.broadcast_to(tau, (1, 128))
        return carry

    lax.fori_loop(0, 8, one_step, 0)
    if base + 8 == width:
        return

    def couple(step, carry):
        column = jnp.sum(vectors[base:base + 8, :] * vectors[pl.ds(base + step, 1), :], axis=1, keepdims=True)
        inner[step] = jnp.broadcast_to(column, (8, 128))
        return carry

    lax.fori_loop(0, 8, couple, 0, unroll=True)

    def trail(group, carry):
        rows = pl.ds(pl.multiple_of(group * 8, 8), 8)
        rest = work[rows, :]
        dots = [jnp.sum(rest * vectors[base + k:base + k + 1, :], axis=1, keepdims=True) for k in range(8)]
        weights = []
        for k in range(8):
            value = dots[k]
            for i in range(k):
                value = value - weights[i] * inner[k, i:i + 1, :]
            weights.append(value * taus[base + k:base + k + 1, :])
        for k in range(8):
            rest = rest - weights[k][:, 0:1] * vectors[base + k:base + k + 1, :]
        work[rows, :] = rest
        return carry

    lax.fori_loop(base // 8 + 1, width // 8, trail, 0, unroll=True)


def triangle(vectors, taus, factor_ref):
    width = vectors.shape[0]
    rows = vectors[...]
    gram = lax.dot_general(rows, rows, (((1,), (1,)), ((), ())), precision=HIGH, preferred_element_type=jnp.float32)
    across = lax.broadcasted_iota(jnp.int32, (width, width), 1)
    down = lax.broadcasted_iota(jnp.int32, (width, width), 0)
    factor = jnp.where(across == down, taus[:, 0:1], 0.0)
    span = 1
    while span < width:
        pick = (down // span + 1 == across // span) & (across // (2 * span) == down // (2 * span))
        middle = jnp.dot(factor, jnp.where(pick, gram, 0.0), precision=HIGH, preferred_element_type=jnp.float32)
        factor = factor - jnp.dot(middle, factor, precision=HIGH, preferred_element_type=jnp.float32)
        span *= 2
    factor_ref[...] = factor


def halves_of(value):
    high = value.astype(jnp.bfloat16)
    return high, (value - high.astype(jnp.float32)).astype(jnp.bfloat16)


def whole_kernel(
    total, library_ref, scale_ref, updated_ref, own_ref,
    whole, left, prod, code_a, code_c, land_a, land_b, land_c,
    head_raw, heads, part, landed, summed, gathered, crossed, work, vectors, taus, inner_dots, factor,
    sample_dots, stacked, thin,
    plane_send, plane_recv, own_sem, left_send, left_recv, z_send, z_recv,
    head_send, head_recv, sum_send, sum_recv, core_send, core_recv,
):
    me, core = lax.axis_index("rows"), lax.axis_index("grid")
    far, near = left.shape[0], 4
    place, level = lax.rem(me, near), me // near
    samples = library_ref.shape[0]
    size = left.shape[1]
    block = library_ref.shape[1]
    width = work.shape[0]
    chunk = size // 2
    buddy = level + 1 - 2 * lax.rem(level, 2)
    base = 2 * (1 - level // 2)
    inner = lax.rem(level + 1, far) // 2 == 1
    outer = lax.rem(level + 1, far) // 2 == 0
    other = (me, 1 - core)
    full = jnp.float32

    def chip(mask):
        return (level * near + flip(place, mask), core)

    def floor(which):
        return (which * near + place, core)

    def beside(step):
        return lax.rem(level + step, far)

    barrier = pltpu.get_barrier_semaphore()
    for target in (chip(1), chip(2), chip(3), floor(beside(1)), floor(beside(2)), floor(beside(3)), other):
        pl.semaphore_signal(barrier, inc=1, device_id=target, device_id_type=MESH)
    pl.semaphore_wait(barrier, 7)

    def columns(zz, group):
        return pl.ds(pl.multiple_of((zz * near + group) * size, size), size)

    def spot(zz, r, source):
        return whole.at[zz * near + r, pl.ds(source * samples, samples)]

    def item(mask, k):
        kind, zz, r = ITEMS[mask][k]
        if kind == "own":
            source = library_ref.at[:, columns(zz, flip(place, r ^ mask))]
            target = spot(zz, r, mask)
        else:
            source = spot(zz, r ^ mask, 3 ^ mask)
            target = spot(zz, r, 3)
        return remote(source, target, plane_send.at[mask - 1, k], plane_recv.at[mask - 1, k], chip(mask))

    seen, sent = set(), []

    def arrive(mask, k):
        if (mask, k) not in seen:
            seen.add((mask, k))
            item(mask, k).wait_recv()

    def send(mask, k):
        kind, zz, r = ITEMS[mask][k]
        if kind == "fwd":
            arrive(3 ^ mask, ITEMS[3 ^ mask].index(("own", zz, r ^ mask)))
        item(mask, k).start()
        sent.append((mask, k))

    def both(action, k):
        action(1, k)
        action(2, k)

    copies = []
    for zz in range(2):
        for r in range(4):
            copies.append(pltpu.make_async_copy(
                library_ref.at[:, columns(zz, flip(place, r))], spot(zz, r, 0), own_sem.at[zz * near + r]))
    head_copy = pltpu.make_async_copy(library_ref.at[:, 0:128], head_raw, own_sem.at[8])
    head_copy.start()
    copies[0].start()
    copies[near].start()
    for k in range(3):
        both(send, k)
    for index, copy in enumerate(copies):
        if index % near:
            copy.start()

    placed = set()

    def landed_own(zz, r):
        if (zz, r) not in placed:
            placed.add((zz, r))
            copies[zz * near + r].wait()

    def head(mask):
        return remote(heads.at[:, 0:samples], heads.at[:, mask * samples:(mask + 1) * samples],
                      head_send.at[mask], head_recv.at[mask], chip(mask))

    def head_over():
        return remote(heads, heads, head_send.at[0], head_recv.at[0], other)

    head_copy.wait()

    @pl.when(core == 0)
    def _():
        heads[:, 0:samples] = head_raw[...].T[0:width, :]
        for mask in (3, 1, 2):
            head(mask).start()

    def piece(zz, source, half):
        target = left.at[2 * half + zz, :, pl.ds(source * samples, samples)]
        index = zz * near + source
        return remote(target, target, left_send.at[index], left_recv.at[index], other)

    def turn(zz, source):
        left[2 * core + zz, :, source * samples:(source + 1) * samples] = (
            whole[zz * near, source * samples:(source + 1) * samples, :].T
        )
        piece(zz, source, core).start()

    for zz in range(2):
        landed_own(zz, 0)
        turn(zz, 0)
    both(arrive, 0)
    turn(0, 1)
    turn(0, 2)
    both(arrive, 1)
    both(send, 3)
    both(arrive, 2)
    both(send, 4)
    turn(1, 1)
    turn(1, 2)

    @pl.when(core == 0)
    def _():
        for mask in (1, 2, 3):
            head(mask).wait_recv()
        head_over().start()

    both(arrive, 3)
    both(send, 5)
    both(send, 6)
    turn(0, 3)
    turn(1, 3)

    @pl.when(core == 1)
    def _():
        head_over().wait_recv()

    def scatter(which, step):
        peer = beside(step)
        return remote(part.at[which, peer], landed.at[which, step], sum_send.at[which, 0, step],
                      sum_recv.at[which, 0, step], floor(peer))

    def spread(which, step, arriving=False):
        spot_of = summed.at[which, beside(far - step)] if arriving else summed.at[which, level]
        return remote(spot_of, spot_of, sum_send.at[which, 1, step], sum_recv.at[which, 1, step], floor(beside(step)))

    def fan(which, mask):
        return remote(summed.at[which], gathered.at[which, mask], sum_send.at[which, 2, mask],
                      sum_recv.at[which, 2, mask], chip(mask))

    def begin_sum(which):
        for step in (2, 1, 3):
            scatter(which, step).start()

    def add_up(which):
        value = part[which, level]
        for step in range(1, far):
            scatter(which, step).wait_recv()
            value = value + landed[which, step]
        summed[which, level] = value
        for step in (2, 1, 3):
            spread(which, step).start()

    def fan_out(which):
        for step in range(1, far):
            spread(which, step, True).wait_recv()
        for mask in (3, 1, 2):
            fan(which, mask).start()
        gathered[which, 0] = summed[which]

    def fan_in(which):
        for mask in range(1, near):
            fan(which, mask).wait_recv()

    def end_sum(which):
        for step in range(1, far):
            scatter(which, step).wait_send()
            spread(which, step).wait_send()
        for mask in range(1, near):
            fan(which, mask).wait_send()

    for zz in range(2):
        value = jnp.dot(heads[...], whole[zz * near], preferred_element_type=full)
        part[0, 2 * zz] = value[:, 0:chunk]
        part[0, 2 * zz + 1] = value[:, chunk:size]
    begin_sum(0)

    def share(t, kind, which=0):
        if kind == "a":
            return remote(code_a.at[t], land_a.at[t], z_send.at[t, 0], z_recv.at[t, 0], floor(buddy))
        if kind == "c":
            return remote(code_c.at[t, which], land_c.at[t, which], z_send.at[t, 1 + which],
                          z_recv.at[t, 1 + which], floor(buddy))
        return remote(code_c.at[t, which], land_b.at[t], z_send.at[t, 1 + which], z_recv.at[t, 3],
                      floor(base + which))

    def combine(t):
        @pl.when(inner)
        def _():
            def one(which, carry):
                share(t, "c", which).wait_recv()
                encode(prod[t, base + which] + decode(land_c.at[t, which]), code_c.at[t, which])
                share(t, "b", which).start()
                return carry

            lax.fori_loop(0, 2, one, 0)

    def multiply(t):
        zz, r = STEPS[t]
        for k in range(READY[t]):
            both(arrive, k)
        landed_own(zz, r)

        def product(target, carry):
            prod[t, target] = jnp.dot(left[target], whole[zz * near + r], preferred_element_type=full)
            return carry

        lax.fori_loop(0, far, product, 0)

        @pl.when(outer)
        def _():
            def one(which, carry):
                encode(prod[t, base + which], code_c.at[t, which])
                share(t, "c", which).start()
                return carry

            lax.fori_loop(0, 2, one, 0)

        encode(prod[t, buddy], code_a.at[t])
        if t:
            share(t - 1, "a").start()
        if t == len(STEPS) - 1:
            share(t, "a").start()

    for zz in range(2):
        for source in range(4):
            piece(zz, source, 1 - core).wait_recv()
    multiply(0)
    add_up(0)
    both(send, 7)
    multiply(1)
    fan_out(0)
    multiply(2)
    both(send, 8)
    both(send, 9)
    combine(0)
    fan_in(0)

    def over(which):
        if which == 0:
            return remote(gathered.at[0], crossed, core_send.at[0], core_recv.at[0], other)
        return remote(sample_dots.at[0], sample_dots.at[1], core_send.at[1], core_recv.at[1], other)

    over(0).start()
    multiply(3)
    combine(1)
    both(send, 10)
    both(send, 11)
    over(0).wait_recv()

    first = jnp.broadcast_to(scale_ref[:, 0:128], (8, 128)).T[0:width, 0:1] * (1.0 / total)
    for mask in range(near):
        for k in range(4):
            column = ((k // 2) * near + flip(place, mask)) * size + (k % 2) * chunk
            for side, half in ((0, core), (1, 1 - core)):
                cols = pl.ds(pl.multiple_of(half * block + column, chunk), chunk)
                value = gathered[0, mask, k] if side == 0 else crossed[mask, k]
                work[:, cols] = value * (first * scale_ref[:, cols])

    for group in range(width // 8):
        reflect_group(8 * group, work, vectors, taus, inner_dots)
        if group == 2:
            combine(2)
        if group == 4:
            combine(3)
        if group == 5:
            multiply(4)
        if group == 6:
            multiply(5)

    def dots(zz, r):
        cols = columns(zz, flip(place, r))
        there = pl.ds(pl.multiple_of(core * block + (zz * near + flip(place, r)) * size, size), size)
        value = vectors[:, there] * scale_ref[:, there]
        high, low = halves_of(value)
        thin[zz * near + r] = jnp.concatenate([high, low], axis=0).T

    for zz in range(2):
        for r in range(4):
            dots(zz, r)
            landed_own(zz, r)
    for k in range(12):
        both(arrive, k)

    def gather_dots(source, carry):
        rows = pl.ds(pl.multiple_of(source * samples, samples), samples)
        value = jnp.dot(whole[0, rows, :], thin[0], preferred_element_type=full)
        for index in range(1, 2 * near):
            value = value + jnp.dot(whole[index, rows, :], thin[index], preferred_element_type=full)
        turned = value.T
        sample_dots[0, :, rows] = turned[0:width, :] + turned[width:2 * width, :]
        return carry

    lax.fori_loop(0, near, gather_dots, 0)
    over(1).start()
    multiply(6)
    triangle(vectors, taus, factor)
    combine(4)
    over(1).wait_recv()
    value = lax.dot_general(
        factor[...], sample_dots[0] + sample_dots[1], (((0,), (0,)), ((), ())), precision=HIGH,
        preferred_element_type=full)
    high, low = halves_of(value)
    stacked[0:width, :] = high
    stacked[width:2 * width, :] = low
    for zz in range(2):
        value = jnp.dot(stacked[...], whole[zz * near], preferred_element_type=full)
        value = value[0:width, :] + value[width:2 * width, :]
        part[1, 2 * zz] = value[:, 0:chunk]
        part[1, 2 * zz + 1] = value[:, chunk:size]
    begin_sum(1)
    multiply(7)
    combine(5)
    add_up(1)
    combine(6)
    fan_out(1)

    mine = pl.ds(pl.multiple_of(me * size, size), size)
    ours = vectors[:, mine]
    own_ref[...] = ours.T
    high, low = halves_of(ours)
    thin_rows = jnp.concatenate([high, high, low, low], axis=0).T
    row_scale = jnp.broadcast_to(scale_ref[:, mine], (8, size)).T[:, 0:1] * (1.0 / total)
    fan_in(1)
    combine(7)

    for t, (zz, r) in enumerate(STEPS):
        cols = columns(zz, flip(place, r))
        there = pl.ds(pl.multiple_of(core * block + (zz * near + flip(place, r)) * size, size), size)
        scale = scale_ref[:, there]
        value = jnp.concatenate([gathered[1, r, 2 * zz], gathered[1, r, 2 * zz + 1]], axis=1)
        high, low = halves_of(value * (scale * (1.0 / total)))
        change = jnp.dot(thin_rows, jnp.concatenate([high, low, high, low], axis=0), preferred_element_type=full)
        share(t, "a").wait_recv()
        share(t, "b").wait_recv()
        value = prod[t, level] + decode(land_a.at[t]) + decode(land_b.at[t])
        updated_ref[:, cols] = value * (row_scale * scale) - change

    for mask, k in sent:
        item(mask, k).wait_send()
    for zz in range(2):
        for source in range(4):
            piece(zz, source, core).wait_send()
    for t in range(len(STEPS)):
        share(t, "a").wait_send()
        for which in range(2):
            share(t, "c", which).wait_send()
    end_sum(0)
    end_sum(1)
    over(0).wait_send()
    over(1).wait_send()

    @pl.when(core == 0)
    def _():
        for mask in (1, 2, 3):
            head(mask).wait_send()
        head_over().wait_send()


def whole_update(library, col_scale, far):
    samples, block = library.shape
    near, cores = 4, 2
    columns = block * cores
    size = columns // (near * far)
    steps = block // size
    half, full = jnp.bfloat16, jnp.float32
    coded = (size + 16, size)
    dma = pltpu.SemaphoreType.DMA
    vmem = pl.BlockSpec(memory_space=pltpu.VMEM)
    small = (PANEL, size // 2)
    return pl.pallas_call(
        functools.partial(whole_kernel, samples * near * far),
        out_shape=(jax.ShapeDtypeStruct((size, block), full), jax.ShapeDtypeStruct((size, PANEL), full)),
        in_specs=[pl.BlockSpec(memory_space=pl.ANY), vmem],
        out_specs=(vmem, vmem),
        scratch_shapes=[
            pltpu.VMEM((steps, near * samples, size), half), pltpu.VMEM((far, size, near * samples), half),
            pltpu.VMEM((steps, far, size, size), full),
            pltpu.VMEM((steps,) + coded, half), pltpu.VMEM((steps, 2) + coded, half),
            pltpu.VMEM((steps,) + coded, half), pltpu.VMEM((steps,) + coded, half),
            pltpu.VMEM((steps, 2) + coded, half),
            pltpu.VMEM((samples, 128), half), pltpu.VMEM((PANEL, near * samples), half),
            pltpu.VMEM((2, far) + small, full), pltpu.VMEM((2, far) + small, full),
            pltpu.VMEM((2, far) + small, full), pltpu.VMEM((2, near, far) + small, full),
            pltpu.VMEM((near, far) + small, full),
            pltpu.VMEM((PANEL, columns), full), pltpu.VMEM((PANEL, columns), full),
            pltpu.VMEM((PANEL, 128), full), pltpu.VMEM((8, 8, 128), full), pltpu.VMEM((PANEL, PANEL), full),
            pltpu.VMEM((2, PANEL, near * samples), full), pltpu.VMEM((2 * PANEL, near * samples), half),
            pltpu.VMEM((steps, size, 2 * PANEL), half),
            dma((2, 12)), dma((2, 12)), dma((9,)), dma((8,)), dma((8,)), dma((steps, 3)), dma((steps, 4)),
            dma((4,)), dma((4,)), dma((2, 3, 4)), dma((2, 3, 4)), dma((2,)), dma((2,)),
        ],
        compiler_params=pltpu.CompilerParams(
            vmem_limit_bytes=56 << 20, collective_id=1, has_side_effects=True
        ),
        cost_estimate=pl.CostEstimate(flops=12_000_000_000, bytes_accessed=10_000_000, transcendentals=0),
    )(library, col_scale)


def per_device(library, col_scale):
    rows_dev, col_block = library.shape
    count_rows = lax.axis_size("rows")
    count_grid = lax.axis_size("grid")
    columns = col_block * count_grid
    row_block = columns // count_rows
    total = rows_dev * count_rows
    near = 1
    while near * near < count_rows:
        near *= 2
    far = count_rows // near
    if count_rows == 16 and count_grid == 2 and row_block % 256 == 0 and rows_dev % 128 == 0:
        return whole_update(library, col_scale[None, :], 4)
    grid_place = lax.axis_index("grid")
    rows_place = lax.axis_index("rows")
    near_groups = [[f * near + n for n in range(near)] for f in range(far)]
    far_groups = [[f * near + n for f in range(far)] for n in range(near)]
    own_scale = lax.dynamic_slice_in_dim(col_scale, grid_place * col_block, col_block)

    head = lax.all_gather(library[:, :PANEL], "grid", axis=0)[0]
    panel_part = lax.dot_general(
        head, library, (((0,), (0,)), ((), ())), preferred_element_type=jnp.float32
    )
    panel_part = panel_part * (col_scale[:PANEL, None] * own_scale[None, :] / total)
    vectors, mixed = panel_chain(panel_part, library, own_scale[None, :], count_rows, count_grid)
    mixed = mixed / total

    whole = lax.all_gather(library, "rows", axis=0, tiled=True, axis_index_groups=near_groups)
    whole, vectors, mixed = lax.optimization_barrier((whole, vectors, mixed))
    place = rows_place % near
    blocks = whole.T.reshape(far // count_grid, near, row_block, near * rows_dev)
    left = lax.dynamic_index_in_dim(blocks, place, 1, keepdims=False)
    left = left.reshape(far // count_grid * row_block, near * rows_dev)
    left = lax.all_gather(left, "grid", axis=0, tiled=True)
    product = lax.dot_general(
        left, whole, (((1,), (0,)), ((), ())), preferred_element_type=jnp.float32
    )
    gram = lax.psum_scatter(
        product, "rows", scatter_dimension=0, tiled=True, axis_index_groups=far_groups
    )
    row_scale = lax.dynamic_slice_in_dim(col_scale, rows_place * row_block, row_block)

    own_vectors = lax.dynamic_slice_in_dim(vectors, rows_place * row_block, row_block, 1).T
    gram = gram * (row_scale[:, None] * own_scale[None, :] / total)
    updated = gram - jnp.dot(own_vectors, mixed, precision=HIGH)
    return (updated, own_vectors)


def solution(mesh):
    return jax.shard_map(
        per_device,
        mesh=mesh,
        in_specs=(P("rows", "grid"), P()),
        out_specs=(P("rows", "grid"), P("rows", None)),
        check_vma=False,
    )
```

```python
import functools

import jax
import jax.numpy as jnp
from jax import lax
from jax.experimental import pallas as pl
from jax.experimental.pallas import tpu as pltpu
from jax.sharding import PartitionSpec as P

PANEL = 64
HIGH = lax.Precision.HIGHEST
MESH = pl.DeviceIdType.MESH


def reflect(vectors_ref, weights_ref, work, inner, taus):
    width, size = work.shape
    lane = lax.broadcasted_iota(jnp.int32, (1, size), 1)
    for base in range(0, width, 8):

        def one_step(step, carry, base=base):
            place = base + step
            row = work[pl.ds(place, 1), :]
            row = jnp.where(lane >= place, row, 0.0)
            pivot = jnp.sum(jnp.where(lane == place, row, 0.0), axis=1, keepdims=True)
            length = jnp.sqrt(jnp.sum(row * row, axis=1, keepdims=True))
            signed = jnp.where(pivot >= 0.0, length, -length)
            vector = row + jnp.where(lane == place, signed, 0.0)
            tau = 1.0 / (length * (length + jnp.abs(pivot)))
            rest = work[base:, :]
            project = jnp.sum(rest * vector, axis=1, keepdims=True)
            work[base:, :] = rest - (tau * project) * vector
            vectors_ref[pl.ds(place, 1), :] = vector
            taus[pl.ds(place, 1), :] = jnp.broadcast_to(tau, (1, 128))
            return carry

        lax.fori_loop(0, 8, one_step, 0)
    vectors = vectors_ref[...]
    inner[...] = lax.dot_general(
        vectors, vectors, (((1,), (1,)), ((), ())), precision=HIGH, preferred_element_type=jnp.float32
    )
    across = lax.broadcasted_iota(jnp.int32, (width, width), 1)
    down = lax.broadcasted_iota(jnp.int32, (width, 1), 0)

    def factor_step(place, factor):
        tau = taus[pl.ds(place, 1), 0:1]
        coupling = jnp.where(across < place, inner[pl.ds(place, 1), :] * factor, 0.0)
        column = -tau * jnp.sum(coupling, axis=1, keepdims=True)
        column = column + jnp.where(down == place, tau, 0.0)
        return jnp.where(across == place, column, factor)

    factor = lax.fori_loop(0, width, factor_step, jnp.zeros((width, width), jnp.float32))
    weights_ref[...] = lax.dot_general(
        factor, vectors, (((0,), (0,)), ((), ())), precision=HIGH, preferred_element_type=jnp.float32
    )


def remote(source, target, send, recv, place):
    return pltpu.make_async_remote_copy(
        src_ref=source, dst_ref=target, send_sem=send, recv_sem=recv,
        device_id=place, device_id_type=pl.DeviceIdType.MESH,
    )


def sum_rows(count, part, landed, out, sems):
    me, core = lax.axis_index("rows"), lax.axis_index("grid")
    send, recv, send_back, recv_back = sems

    def scatter(step):
        peer = lax.rem(me + step, count)
        return remote(part.at[peer], landed.at[step], send.at[step], recv.at[step], (peer, core))

    def spread(step):
        peer = lax.rem(me + step, count)
        return remote(out.at[me], out.at[me], send_back.at[step], recv_back.at[step], (peer, core))

    def arrival(step):
        peer = lax.rem(me + count - step, count)
        return remote(out.at[peer], out.at[peer], send_back.at[step], recv_back.at[step], (peer, core))

    def loop(action):
        def body(step, carry):
            action(step)
            return carry
        lax.fori_loop(1, count, body, 0)

    loop(lambda step: scatter(step).start())
    loop(lambda step: scatter(step).wait_recv())
    total = part[me]
    for step in range(1, count):
        total = total + landed[step]
    out[me] = total
    loop(lambda step: spread(step).start())
    loop(lambda step: arrival(step).wait_recv())
    loop(lambda step: scatter(step).wait_send())
    loop(lambda step: spread(step).wait_send())


def panel_kernel(
    count, cores, part_ref, library_ref, scale_ref, vectors_ref, mixed_ref,
    part, landed, gathered, part_two, landed_two, gathered_two, halves,
    weights, work, inner, taus, row_sems, row_sems_two, core_sems, half_sems,
):
    me, core = lax.axis_index("rows"), lax.axis_index("grid")
    width, block = part_ref.shape
    per = width // count
    barrier = pltpu.get_barrier_semaphore()

    def greet(step, carry):
        pl.semaphore_signal(
            barrier, inc=1, device_id=(lax.rem(me + step, count), core), device_id_type=pl.DeviceIdType.MESH
        )
        return carry

    lax.fori_loop(1, count, greet, 0)
    for step in range(1, cores):
        pl.semaphore_signal(
            barrier, inc=1, device_id=(me, lax.rem(core + step, cores)), device_id_type=pl.DeviceIdType.MESH
        )
    for place in range(count):
        part[place] = part_ref[place * per:(place + 1) * per, :]
    pl.semaphore_wait(barrier, count + cores - 2)

    sum_rows(count, part, landed, gathered.at[core], [row_sems.at[k] for k in range(4)])
    shares = []
    for step in range(1, cores):
        peer = lax.rem(core + step, cores)
        shares.append(
            remote(gathered.at[core], gathered.at[core], core_sems.at[0, step], core_sems.at[1, step], (me, peer))
        )
        shares[-1].start()
    for step in range(1, cores):
        peer = lax.rem(core + cores - step, cores)
        remote(
            gathered.at[peer], gathered.at[peer], core_sems.at[0, step], core_sems.at[1, step], (me, peer)
        ).wait_recv()
    for share in shares:
        share.wait_send()
    for half in range(cores):
        for place in range(count):
            work[place * per:(place + 1) * per, half * block:(half + 1) * block] = gathered[half, place]

    reflect(vectors_ref, weights, work, inner, taus)

    step_cols = min(block, 512)
    halves[0] = jnp.zeros_like(halves[0])
    for start in range(0, block, step_cols):
        cols = slice(start, start + step_cols)
        own = weights[:, pl.ds(pl.multiple_of(core * block + start, 128), step_cols)] * scale_ref[:, cols]
        halves[0] += lax.dot_general(
            own, library_ref[:, cols].astype(jnp.float32), (((1,), (1,)), ((), ())),
            precision=HIGH, preferred_element_type=jnp.float32,
        )
    shares = []
    for step in range(1, cores):
        peer = lax.rem(core + step, cores)
        shares.append(
            remote(halves.at[0], halves.at[step], half_sems.at[0, step], half_sems.at[1, step], (me, peer))
        )
        shares[-1].start()
    for share in shares:
        share.wait()
    summed = halves[0]
    for step in range(1, cores):
        summed = summed + halves[step]
    for start in range(0, block, step_cols):
        cols = slice(start, start + step_cols)
        chunk = jnp.dot(
            summed, library_ref[:, cols].astype(jnp.float32), precision=HIGH, preferred_element_type=jnp.float32
        )
        for place in range(count):
            part_two[place, :, cols] = chunk[place * per:(place + 1) * per, :]
    sum_rows(count, part_two, landed_two, gathered_two, [row_sems_two.at[k] for k in range(4)])
    for place in range(count):
        mixed_ref[place * per:(place + 1) * per, :] = gathered_two[place] * scale_ref[...]


def panel_chain(part, library, scale, count, cores):
    width, block = part.shape
    rows_dev = library.shape[0]
    per = width // count
    size = block * cores
    real = jnp.float32
    slices = pltpu.VMEM((count, per, block), real)
    return pl.pallas_call(
        functools.partial(panel_kernel, count, cores),
        out_shape=(jax.ShapeDtypeStruct((width, size), real), jax.ShapeDtypeStruct((width, block), real)),
        in_specs=[pl.BlockSpec(memory_space=pltpu.VMEM)] * 3,
        out_specs=(pl.BlockSpec(memory_space=pltpu.VMEM),) * 2,
        scratch_shapes=[
            slices, slices, pltpu.VMEM((cores, count, per, block), real),
            slices, slices, slices, pltpu.VMEM((cores, width, rows_dev), real),
            pltpu.VMEM((width, size), real), pltpu.VMEM((width, size), real),
            pltpu.VMEM((width, width), real), pltpu.VMEM((width, 128), real),
            pltpu.SemaphoreType.DMA((4, count)), pltpu.SemaphoreType.DMA((4, count)),
            pltpu.SemaphoreType.DMA((2, cores)), pltpu.SemaphoreType.DMA((2, cores)),
        ],
        compiler_params=pltpu.CompilerParams(
            vmem_limit_bytes=32 << 20, collective_id=0, has_side_effects=True
        ),
        cost_estimate=pl.CostEstimate(flops=20_000_000_000, bytes_accessed=200_000_000, transcendentals=0),
    )(part, library, scale)


X_ITEMS = (
    ("own", 0, 0), ("own", 1, 2), ("own", 1, 0), ("fwd", 0, 0), ("own", 0, 1), ("fwd", 0, 1),
    ("own", 1, 3), ("own", 1, 1), ("fwd", 0, 2), ("own", 0, 2), ("fwd", 0, 3), ("own", 0, 3),
)
Y_ITEMS = (
    ("own", 0, 0), ("own", 0, 1), ("own", 1, 0), ("fwd", 1, 0), ("own", 1, 2), ("fwd", 1, 2),
    ("own", 0, 3), ("own", 0, 2), ("fwd", 1, 1), ("own", 1, 1), ("fwd", 1, 3), ("own", 1, 3),
)
ITEMS = {1: X_ITEMS, 2: Y_ITEMS}
STEPS = ((0, 0), (1, 0), (0, 1), (1, 2), (0, 2), (1, 1), (0, 3), (1, 3))
READY = (4, 4, 6, 6, 10, 10, 12, 12)
TOP = 2.0 ** 15.5
LEAST = 2.0 ** -125


def flip(place, mask):
    low, high = lax.rem(place, 2), place // 2
    low = 1 - low if mask & 1 else low
    high = 1 - high if mask & 2 else high
    return high * 2 + low


def encode(value, target):
    size = value.shape[0]
    peak = jnp.max(jnp.max(jnp.abs(value), axis=0, keepdims=True), axis=1, keepdims=True)
    unit = jnp.maximum(peak, 1e-30).astype(jnp.bfloat16)
    target[size:size + 16, :] = jnp.broadcast_to(unit, (16, value.shape[1]))
    level = value * (TOP / unit.astype(jnp.float32))
    square = level * level
    fourth = square * square
    eighth = fourth * fourth
    target[0:size, :] = jnp.where(level < 0.0, -eighth, eighth).astype(jnp.bfloat16)


def decode(source):
    size = source.shape[0] - 16
    unit = source[size:size + 16, :].astype(jnp.float32)[0:1, 0:1]
    code = source[0:size, :].astype(jnp.float32)
    second = lax.rsqrt(lax.rsqrt(jnp.maximum(jnp.abs(code), LEAST)))
    value = second * lax.rsqrt(second) * (unit * (1.0 / TOP))
    return jnp.where(code < 0.0, -value, value)


def reflect_group(base, work, vectors, taus, inner):
    width, size = work.shape
    lane = lax.broadcasted_iota(jnp.int32, (1, 128), 1)

    def one_step(step, carry):
        place = base + step
        row = work[pl.ds(place, 1), :]
        head, tail = jnp.where(lane >= place, row[:, 0:128], 0.0), row[:, 128:size]
        near = work[base:base + 8, 0:128]
        rest = work[base:base + 8, 128:size]
        square = jnp.sum(head * head, axis=1, keepdims=True) + jnp.sum(tail * tail, axis=1, keepdims=True)
        pivot = jnp.sum(jnp.where(lane == place, head, 0.0), axis=1, keepdims=True)
        project = jnp.sum(near * head, axis=1, keepdims=True) + jnp.sum(rest * tail, axis=1, keepdims=True)
        across = jnp.sum(jnp.where(lane == place, near, 0.0), axis=1, keepdims=True)
        length = jnp.sqrt(square)
        signed = jnp.where(pivot >= 0.0, length, -length)
        tau = 1.0 / (length * (length + jnp.abs(pivot)))
        weight = tau * (project + signed * across)
        head = head + jnp.where(lane == place, signed, 0.0)
        work[base:base + 8, 0:128] = near - weight * head
        work[base:base + 8, 128:size] = rest - weight * tail
        vectors[pl.ds(place, 1), :] = jnp.concatenate([head, tail], axis=1)
        taus[pl.ds(place, 1), :] = jnp.broadcast_to(tau, (1, 128))
        return carry

    lax.fori_loop(0, 8, one_step, 0)
    if base + 8 == width:
        return

    def couple(step, carry):
        column = jnp.sum(vectors[base:base + 8, :] * vectors[pl.ds(base + step, 1), :], axis=1, keepdims=True)
        inner[step] = jnp.broadcast_to(column, (8, 128))
        return carry

    lax.fori_loop(0, 8, couple, 0, unroll=True)

    def trail(group, carry):
        rows = pl.ds(pl.multiple_of(group * 8, 8), 8)
        rest = work[rows, :]
        dots = [jnp.sum(rest * vectors[base + k:base + k + 1, :], axis=1, keepdims=True) for k in range(8)]
        weights = []
        for k in range(8):
            value = dots[k]
            for i in range(k):
                value = value - weights[i] * inner[k, i:i + 1, :]
            weights.append(value * taus[base + k:base + k + 1, :])
        for k in range(8):
            rest = rest - weights[k][:, 0:1] * vectors[base + k:base + k + 1, :]
        work[rows, :] = rest
        return carry

    lax.fori_loop(base // 8 + 1, width // 8, trail, 0, unroll=True)


def triangle(vectors, taus, factor_ref):
    width = vectors.shape[0]
    rows = vectors[...]
    gram = lax.dot_general(rows, rows, (((1,), (1,)), ((), ())), precision=HIGH, preferred_element_type=jnp.float32)
    across = lax.broadcasted_iota(jnp.int32, (width, width), 1)
    down = lax.broadcasted_iota(jnp.int32, (width, width), 0)
    factor = jnp.where(across == down, taus[:, 0:1], 0.0)
    span = 1
    while span < width:
        pick = (down // span + 1 == across // span) & (across // (2 * span) == down // (2 * span))
        middle = jnp.dot(factor, jnp.where(pick, gram, 0.0), precision=HIGH, preferred_element_type=jnp.float32)
        factor = factor - jnp.dot(middle, factor, precision=HIGH, preferred_element_type=jnp.float32)
        span *= 2
    factor_ref[...] = factor


def halves_of(value):
    high = value.astype(jnp.bfloat16)
    return high, (value - high.astype(jnp.float32)).astype(jnp.bfloat16)


def whole_kernel(
    total, library_ref, scale_ref, updated_ref, own_ref,
    whole, left, prod, code_a, code_c, land_a, land_b, land_c,
    head_raw, heads, part, landed, summed, gathered, crossed, work, vectors, taus, inner_dots, factor,
    sample_dots, stacked, thin, sums,
    plane_send, plane_recv, own_sem, left_send, left_recv, z_send, z_recv,
    head_send, head_recv, sum_send, sum_recv, core_send, core_recv,
):
    me, core = lax.axis_index("rows"), lax.axis_index("grid")
    far, near = left.shape[0], 4
    place, level = lax.rem(me, near), me // near
    samples = library_ref.shape[0]
    size = left.shape[1]
    block = library_ref.shape[1]
    width = work.shape[0]
    chunk = size // 2
    buddy = level + 1 - 2 * lax.rem(level, 2)
    base = 2 * (1 - level // 2)
    inner = lax.rem(level + 1, far) // 2 == 1
    outer = lax.rem(level + 1, far) // 2 == 0
    other = (me, 1 - core)
    full = jnp.float32

    def chip(mask):
        return (level * near + flip(place, mask), core)

    def floor(which):
        return (which * near + place, core)

    def beside(step):
        return lax.rem(level + step, far)

    barrier = pltpu.get_barrier_semaphore()
    for target in (chip(1), chip(2), chip(3), floor(beside(1)), floor(beside(2)), floor(beside(3)), other):
        pl.semaphore_signal(barrier, inc=1, device_id=target, device_id_type=MESH)
    pl.semaphore_wait(barrier, 7)

    def columns(zz, group):
        return pl.ds(pl.multiple_of((zz * near + group) * size, size), size)

    def spot(zz, r, source):
        return whole.at[zz * near + r, pl.ds(source * samples, samples)]

    def item(mask, k):
        kind, zz, r = ITEMS[mask][k]
        if kind == "own":
            source = library_ref.at[:, columns(zz, flip(place, r ^ mask))]
            target = spot(zz, r, mask)
        else:
            source = spot(zz, r ^ mask, 3 ^ mask)
            target = spot(zz, r, 3)
        return remote(source, target, plane_send.at[mask - 1, k], plane_recv.at[mask - 1, k], chip(mask))

    seen, sent = set(), []

    def arrive(mask, k):
        if (mask, k) not in seen:
            seen.add((mask, k))
            item(mask, k).wait_recv()

    def send(mask, k):
        kind, zz, r = ITEMS[mask][k]
        if kind == "fwd":
            arrive(3 ^ mask, ITEMS[3 ^ mask].index(("own", zz, r ^ mask)))
        item(mask, k).start()
        sent.append((mask, k))

    def both(action, k):
        action(1, k)
        action(2, k)

    copies = []
    for zz in range(2):
        for r in range(4):
            copies.append(pltpu.make_async_copy(
                library_ref.at[:, columns(zz, flip(place, r))], spot(zz, r, 0), own_sem.at[zz * near + r]))
    head_copy = pltpu.make_async_copy(library_ref.at[:, 0:128], head_raw, own_sem.at[8])
    head_copy.start()
    copies[0].start()
    copies[near].start()
    for k in range(3):
        both(send, k)
    for index, copy in enumerate(copies):
        if index % near:
            copy.start()

    placed = set()

    def landed_own(zz, r):
        if (zz, r) not in placed:
            placed.add((zz, r))
            copies[zz * near + r].wait()

    def head(mask):
        return remote(heads.at[:, 0:samples], heads.at[:, mask * samples:(mask + 1) * samples],
                      head_send.at[mask], head_recv.at[mask], chip(mask))

    def head_over():
        return remote(heads, heads, head_send.at[0], head_recv.at[0], other)

    head_copy.wait()

    @pl.when(core == 0)
    def _():
        heads[:, 0:samples] = head_raw[...].T[0:width, :]
        for mask in (3, 1, 2):
            head(mask).start()

    def piece(zz, source, half):
        target = left.at[2 * half + zz, :, pl.ds(source * samples, samples)]
        index = zz * near + source
        return remote(target, target, left_send.at[index], left_recv.at[index], other)

    def turn(zz, source):
        left[2 * core + zz, :, source * samples:(source + 1) * samples] = (
            whole[zz * near, source * samples:(source + 1) * samples, :].T
        )
        piece(zz, source, core).start()

    for zz in range(2):
        landed_own(zz, 0)
        turn(zz, 0)
    both(arrive, 0)
    turn(0, 1)
    turn(0, 2)
    both(arrive, 1)
    both(send, 3)
    both(arrive, 2)
    both(send, 4)
    turn(1, 1)
    turn(1, 2)

    @pl.when(core == 0)
    def _():
        for mask in (1, 2, 3):
            head(mask).wait_recv()
        head_over().start()

    both(arrive, 3)
    both(send, 5)
    turn(0, 3)
    turn(1, 3)

    @pl.when(core == 1)
    def _():
        head_over().wait_recv()

    def scatter(which, step):
        peer = beside(step)
        return remote(part.at[which, peer], landed.at[which, step], sum_send.at[which, 0, step],
                      sum_recv.at[which, 0, step], floor(peer))

    def spread(which, step, arriving=False):
        spot_of = summed.at[which, beside(far - step)] if arriving else summed.at[which, level]
        return remote(spot_of, spot_of, sum_send.at[which, 1, step], sum_recv.at[which, 1, step], floor(beside(step)))

    def fan(which, mask):
        return remote(summed.at[which], gathered.at[which, mask], sum_send.at[which, 2, mask],
                      sum_recv.at[which, 2, mask], chip(mask))

    def begin_sum(which):
        for step in (2, 1, 3):
            scatter(which, step).start()

    def add_up(which):
        value = part[which, level]
        for step in range(1, far):
            scatter(which, step).wait_recv()
            value = value + landed[which, step]
        summed[which, level] = value
        for step in (2, 1, 3):
            spread(which, step).start()

    def fan_out(which):
        for step in range(1, far):
            spread(which, step, True).wait_recv()
        for mask in (3, 1, 2):
            fan(which, mask).start()
        gathered[which, 0] = summed[which]

    def fan_in(which):
        for mask in range(1, near):
            fan(which, mask).wait_recv()

    def end_sum(which):
        for step in range(1, far):
            scatter(which, step).wait_send()
            spread(which, step).wait_send()
        for mask in range(1, near):
            fan(which, mask).wait_send()

    for zz in range(2):
        value = jnp.dot(heads[...], whole[zz * near], preferred_element_type=full)
        part[0, 2 * zz] = value[:, 0:chunk]
        part[0, 2 * zz + 1] = value[:, chunk:size]
    begin_sum(0)

    def share(t, kind, which=0):
        if kind == "a":
            return remote(code_a.at[t], land_a.at[t], z_send.at[t, 0], z_recv.at[t, 0], floor(buddy))
        if kind == "c":
            return remote(code_c.at[t, which], land_c.at[t, which], z_send.at[t, 1 + which],
                          z_recv.at[t, 1 + which], floor(buddy))
        return remote(code_c.at[t, which], land_b.at[t], z_send.at[t, 1 + which], z_recv.at[t, 3],
                      floor(base + which))

    def combine(t):
        @pl.when(inner)
        def _():
            def one(which, carry):
                share(t, "c", which).wait_recv()
                encode(prod[t, base + which] + decode(land_c.at[t, which]), code_c.at[t, which])
                share(t, "b", which).start()
                return carry

            lax.fori_loop(0, 2, one, 0)

    def multiply(t):
        zz, r = STEPS[t]
        for k in range(READY[t]):
            both(arrive, k)
        landed_own(zz, r)

        def product(target):
            prod[t, target] = jnp.dot(left[target], whole[zz * near + r], preferred_element_type=full)

        def one(which, carry):
            product(base + which)

            @pl.when(outer)
            def _():
                encode(prod[t, base + which], code_c.at[t, which])
                share(t, "c", which).start()

            return carry

        lax.fori_loop(0, 2, one, 0)
        product(buddy)
        encode(prod[t, buddy], code_a.at[t])
        product(level)

    def send_a(t):
        share(t, "a").start()

    for zz in range(2):
        for source in range(4):
            piece(zz, source, 1 - core).wait_recv()
    multiply(0)
    add_up(0)
    multiply(1)
    fan_out(0)
    both(send, 6)
    both(send, 7)
    send_a(0)
    multiply(2)
    combine(0)
    multiply(3)
    send_a(1)
    fan_in(0)

    def over(which):
        if which == 0:
            return remote(gathered.at[0], crossed, core_send.at[0], core_recv.at[0], other)
        return remote(sample_dots.at[0], sample_dots.at[1], core_send.at[1], core_recv.at[1], other)

    over(0).start()
    combine(1)
    send_a(2)
    send_a(3)
    over(0).wait_recv()

    first = jnp.broadcast_to(scale_ref[:, 0:128], (8, 128)).T[0:width, 0:1] * (1.0 / total)
    for mask in range(near):
        for k in range(4):
            column = ((k // 2) * near + flip(place, mask)) * size + (k % 2) * chunk
            for side, half in ((0, core), (1, 1 - core)):
                cols = pl.ds(pl.multiple_of(half * block + column, chunk), chunk)
                value = gathered[0, mask, k] if side == 0 else crossed[mask, k]
                work[:, cols] = value * (first * scale_ref[:, cols])

    for group in range(width // 8):
        reflect_group(8 * group, work, vectors, taus, inner_dots)
        if group == 1:
            both(send, 8)
            both(send, 9)
        if group == 2:
            combine(2)
        if group == 3:
            both(send, 10)
            both(send, 11)
        if group == 4:
            combine(3)

    def dots(zz, r):
        cols = columns(zz, flip(place, r))
        there = pl.ds(pl.multiple_of(core * block + (zz * near + flip(place, r)) * size, size), size)
        value = vectors[:, there] * scale_ref[:, there]
        high, low = halves_of(value)
        thin[zz * near + r] = jnp.concatenate([high, low], axis=0).T

    for zz in range(2):
        for r in range(4):
            dots(zz, r)
    multiply(4)
    multiply(5)
    send_a(4)
    triangle(vectors, taus, factor)

    def gather_dots(blocks, first_time):
        def one(source, carry):
            rows = pl.ds(pl.multiple_of(source * samples, samples), samples)
            value = jnp.dot(whole[blocks[0], rows, :], thin[blocks[0]], preferred_element_type=full)
            for index in blocks[1:]:
                value = value + jnp.dot(whole[index, rows, :], thin[index], preferred_element_type=full)
            if first_time:
                sums[rows, :] = value
            else:
                turned = (sums[rows, :] + value).T
                sample_dots[0, :, rows] = turned[0:width, :] + turned[width:2 * width, :]
            return carry

        lax.fori_loop(0, near, one, 0)

    order = [zz * near + r for zz, r in STEPS]
    gather_dots(order[:6], True)
    combine(4)
    for k in range(12):
        both(arrive, k)
    for zz, r in STEPS[6:]:
        landed_own(zz, r)
    gather_dots(order[6:], False)
    over(1).start()
    multiply(6)
    over(1).wait_recv()
    value = lax.dot_general(
        factor[...], sample_dots[0] + sample_dots[1], (((0,), (0,)), ((), ())), precision=HIGH,
        preferred_element_type=full)
    high, low = halves_of(value)
    stacked[0:width, :] = high
    stacked[width:2 * width, :] = low
    for zz in range(2):
        value = jnp.dot(stacked[...], whole[zz * near], preferred_element_type=full)
        value = value[0:width, :] + value[width:2 * width, :]
        part[1, 2 * zz] = value[:, 0:chunk]
        part[1, 2 * zz + 1] = value[:, chunk:size]
    begin_sum(1)
    multiply(7)
    combine(5)
    add_up(1)
    send_a(5)
    send_a(6)
    send_a(7)
    combine(6)
    fan_out(1)

    mine = pl.ds(pl.multiple_of(me * size, size), size)
    ours = vectors[:, mine]
    own_ref[...] = ours
    high, low = halves_of(ours)
    thin_rows = jnp.concatenate([high, high, low, low], axis=0).T
    row_scale = jnp.broadcast_to(scale_ref[:, mine], (8, size)).T[:, 0:1] * (1.0 / total)
    combine(7)
    fan_in(1)

    for t, (zz, r) in enumerate(STEPS):
        cols = columns(zz, flip(place, r))
        there = pl.ds(pl.multiple_of(core * block + (zz * near + flip(place, r)) * size, size), size)
        scale = scale_ref[:, there]
        value = jnp.concatenate([gathered[1, r, 2 * zz], gathered[1, r, 2 * zz + 1]], axis=1)
        high, low = halves_of(value * (scale * (1.0 / total)))
        change = jnp.dot(thin_rows, jnp.concatenate([high, low, high, low], axis=0), preferred_element_type=full)
        share(t, "a").wait_recv()
        share(t, "b").wait_recv()
        value = prod[t, level] + decode(land_a.at[t]) + decode(land_b.at[t])
        updated_ref[:, cols] = value * (row_scale * scale) - change

    for mask, k in sent:
        item(mask, k).wait_send()
    for zz in range(2):
        for source in range(4):
            piece(zz, source, core).wait_send()
    for t in range(len(STEPS)):
        share(t, "a").wait_send()
        for which in range(2):
            share(t, "c", which).wait_send()
    end_sum(0)
    end_sum(1)
    over(0).wait_send()
    over(1).wait_send()

    @pl.when(core == 0)
    def _():
        for mask in (1, 2, 3):
            head(mask).wait_send()
        head_over().wait_send()


def whole_update(library, col_scale, far):
    samples, block = library.shape
    near, cores = 4, 2
    columns = block * cores
    size = columns // (near * far)
    steps = block // size
    half, full = jnp.bfloat16, jnp.float32
    coded = (size + 16, size)
    dma = pltpu.SemaphoreType.DMA
    vmem = pl.BlockSpec(memory_space=pltpu.VMEM)
    small = (PANEL, size // 2)
    updated, own = pl.pallas_call(
        functools.partial(whole_kernel, samples * near * far),
        out_shape=(jax.ShapeDtypeStruct((size, block), full), jax.ShapeDtypeStruct((PANEL, size), full)),
        in_specs=[pl.BlockSpec(memory_space=pl.ANY), vmem],
        out_specs=(vmem, vmem),
        scratch_shapes=[
            pltpu.VMEM((steps, near * samples, size), half), pltpu.VMEM((far, size, near * samples), half),
            pltpu.VMEM((steps, far, size, size), full),
            pltpu.VMEM((steps,) + coded, half), pltpu.VMEM((steps, 2) + coded, half),
            pltpu.VMEM((steps,) + coded, half), pltpu.VMEM((steps,) + coded, half),
            pltpu.VMEM((steps, 2) + coded, half),
            pltpu.VMEM((samples, 128), half), pltpu.VMEM((PANEL, near * samples), half),
            pltpu.VMEM((2, far) + small, full), pltpu.VMEM((2, far) + small, full),
            pltpu.VMEM((2, far) + small, full), pltpu.VMEM((2, near, far) + small, full),
            pltpu.VMEM((near, far) + small, full),
            pltpu.VMEM((PANEL, columns), full), pltpu.VMEM((PANEL, columns), full),
            pltpu.VMEM((PANEL, 128), full), pltpu.VMEM((8, 8, 128), full), pltpu.VMEM((PANEL, PANEL), full),
            pltpu.VMEM((2, PANEL, near * samples), full), pltpu.VMEM((2 * PANEL, near * samples), half),
            pltpu.VMEM((steps, size, 2 * PANEL), half), pltpu.VMEM((near * samples, 2 * PANEL), full),
            dma((2, 12)), dma((2, 12)), dma((9,)), dma((8,)), dma((8,)), dma((steps, 3)), dma((steps, 4)),
            dma((4,)), dma((4,)), dma((2, 3, 4)), dma((2, 3, 4)), dma((2,)), dma((2,)),
        ],
        compiler_params=pltpu.CompilerParams(
            vmem_limit_bytes=44 << 20, collective_id=1, has_side_effects=True
        ),
        cost_estimate=pl.CostEstimate(flops=12_000_000_000, bytes_accessed=10_000_000, transcendentals=0),
    )(library, col_scale)
    return updated, own.T


def per_device(library, col_scale):
    rows_dev, col_block = library.shape
    count_rows = lax.axis_size("rows")
    count_grid = lax.axis_size("grid")
    columns = col_block * count_grid
    row_block = columns // count_rows
    total = rows_dev * count_rows
    near = 1
    while near * near < count_rows:
        near *= 2
    far = count_rows // near
    if count_rows == 16 and count_grid == 2 and row_block % 256 == 0 and rows_dev % 128 == 0:
        return whole_update(library, col_scale[None, :], 4)
    grid_place = lax.axis_index("grid")
    rows_place = lax.axis_index("rows")
    near_groups = [[f * near + n for n in range(near)] for f in range(far)]
    far_groups = [[f * near + n for f in range(far)] for n in range(near)]
    own_scale = lax.dynamic_slice_in_dim(col_scale, grid_place * col_block, col_block)

    head = lax.all_gather(library[:, :PANEL], "grid", axis=0)[0]
    panel_part = lax.dot_general(
        head, library, (((0,), (0,)), ((), ())), preferred_element_type=jnp.float32
    )
    panel_part = panel_part * (col_scale[:PANEL, None] * own_scale[None, :] / total)
    vectors, mixed = panel_chain(panel_part, library, own_scale[None, :], count_rows, count_grid)
    mixed = mixed / total

    whole = lax.all_gather(library, "rows", axis=0, tiled=True, axis_index_groups=near_groups)
    whole, vectors, mixed = lax.optimization_barrier((whole, vectors, mixed))
    place = rows_place % near
    blocks = whole.T.reshape(far // count_grid, near, row_block, near * rows_dev)
    left = lax.dynamic_index_in_dim(blocks, place, 1, keepdims=False)
    left = left.reshape(far // count_grid * row_block, near * rows_dev)
    left = lax.all_gather(left, "grid", axis=0, tiled=True)
    product = lax.dot_general(
        left, whole, (((1,), (0,)), ((), ())), preferred_element_type=jnp.float32
    )
    gram = lax.psum_scatter(
        product, "rows", scatter_dimension=0, tiled=True, axis_index_groups=far_groups
    )
    row_scale = lax.dynamic_slice_in_dim(col_scale, rows_place * row_block, row_block)

    own_vectors = lax.dynamic_slice_in_dim(vectors, rows_place * row_block, row_block, 1).T
    gram = gram * (row_scale[:, None] * own_scale[None, :] / total)
    updated = gram - jnp.dot(own_vectors, mixed, precision=HIGH)
    return (updated, own_vectors)


def solution(mesh):
    return jax.shard_map(
        per_device,
        mesh=mesh,
        in_specs=(P("rows", "grid"), P()),
        out_specs=(P("rows", "grid"), P("rows", None)),
        check_vma=False,
    )
```

```python
import functools

import jax
import jax.numpy as jnp
from jax import lax
from jax.experimental import pallas as pl
from jax.experimental.pallas import tpu as pltpu
from jax.sharding import PartitionSpec as P

PANEL = 64
HIGH = lax.Precision.HIGHEST
MESH = pl.DeviceIdType.MESH


def reflect(vectors_ref, weights_ref, work, inner, taus):
    width, size = work.shape
    lane = lax.broadcasted_iota(jnp.int32, (1, size), 1)
    for base in range(0, width, 8):

        def one_step(step, carry, base=base):
            place = base + step
            row = work[pl.ds(place, 1), :]
            row = jnp.where(lane >= place, row, 0.0)
            pivot = jnp.sum(jnp.where(lane == place, row, 0.0), axis=1, keepdims=True)
            length = jnp.sqrt(jnp.sum(row * row, axis=1, keepdims=True))
            signed = jnp.where(pivot >= 0.0, length, -length)
            vector = row + jnp.where(lane == place, signed, 0.0)
            tau = 1.0 / (length * (length + jnp.abs(pivot)))
            rest = work[base:, :]
            project = jnp.sum(rest * vector, axis=1, keepdims=True)
            work[base:, :] = rest - (tau * project) * vector
            vectors_ref[pl.ds(place, 1), :] = vector
            taus[pl.ds(place, 1), :] = jnp.broadcast_to(tau, (1, 128))
            return carry

        lax.fori_loop(0, 8, one_step, 0)
    vectors = vectors_ref[...]
    inner[...] = lax.dot_general(
        vectors, vectors, (((1,), (1,)), ((), ())), precision=HIGH, preferred_element_type=jnp.float32
    )
    across = lax.broadcasted_iota(jnp.int32, (width, width), 1)
    down = lax.broadcasted_iota(jnp.int32, (width, 1), 0)

    def factor_step(place, factor):
        tau = taus[pl.ds(place, 1), 0:1]
        coupling = jnp.where(across < place, inner[pl.ds(place, 1), :] * factor, 0.0)
        column = -tau * jnp.sum(coupling, axis=1, keepdims=True)
        column = column + jnp.where(down == place, tau, 0.0)
        return jnp.where(across == place, column, factor)

    factor = lax.fori_loop(0, width, factor_step, jnp.zeros((width, width), jnp.float32))
    weights_ref[...] = lax.dot_general(
        factor, vectors, (((0,), (0,)), ((), ())), precision=HIGH, preferred_element_type=jnp.float32
    )


def remote(source, target, send, recv, place):
    return pltpu.make_async_remote_copy(
        src_ref=source, dst_ref=target, send_sem=send, recv_sem=recv,
        device_id=place, device_id_type=pl.DeviceIdType.MESH,
    )


def sum_rows(count, part, landed, out, sems):
    me, core = lax.axis_index("rows"), lax.axis_index("grid")
    send, recv, send_back, recv_back = sems

    def scatter(step):
        peer = lax.rem(me + step, count)
        return remote(part.at[peer], landed.at[step], send.at[step], recv.at[step], (peer, core))

    def spread(step):
        peer = lax.rem(me + step, count)
        return remote(out.at[me], out.at[me], send_back.at[step], recv_back.at[step], (peer, core))

    def arrival(step):
        peer = lax.rem(me + count - step, count)
        return remote(out.at[peer], out.at[peer], send_back.at[step], recv_back.at[step], (peer, core))

    def loop(action):
        def body(step, carry):
            action(step)
            return carry
        lax.fori_loop(1, count, body, 0)

    loop(lambda step: scatter(step).start())
    loop(lambda step: scatter(step).wait_recv())
    total = part[me]
    for step in range(1, count):
        total = total + landed[step]
    out[me] = total
    loop(lambda step: spread(step).start())
    loop(lambda step: arrival(step).wait_recv())
    loop(lambda step: scatter(step).wait_send())
    loop(lambda step: spread(step).wait_send())


def panel_kernel(
    count, cores, part_ref, library_ref, scale_ref, vectors_ref, mixed_ref,
    part, landed, gathered, part_two, landed_two, gathered_two, halves,
    weights, work, inner, taus, row_sems, row_sems_two, core_sems, half_sems,
):
    me, core = lax.axis_index("rows"), lax.axis_index("grid")
    width, block = part_ref.shape
    per = width // count
    barrier = pltpu.get_barrier_semaphore()

    def greet(step, carry):
        pl.semaphore_signal(
            barrier, inc=1, device_id=(lax.rem(me + step, count), core), device_id_type=pl.DeviceIdType.MESH
        )
        return carry

    lax.fori_loop(1, count, greet, 0)
    for step in range(1, cores):
        pl.semaphore_signal(
            barrier, inc=1, device_id=(me, lax.rem(core + step, cores)), device_id_type=pl.DeviceIdType.MESH
        )
    for place in range(count):
        part[place] = part_ref[place * per:(place + 1) * per, :]
    pl.semaphore_wait(barrier, count + cores - 2)

    sum_rows(count, part, landed, gathered.at[core], [row_sems.at[k] for k in range(4)])
    shares = []
    for step in range(1, cores):
        peer = lax.rem(core + step, cores)
        shares.append(
            remote(gathered.at[core], gathered.at[core], core_sems.at[0, step], core_sems.at[1, step], (me, peer))
        )
        shares[-1].start()
    for step in range(1, cores):
        peer = lax.rem(core + cores - step, cores)
        remote(
            gathered.at[peer], gathered.at[peer], core_sems.at[0, step], core_sems.at[1, step], (me, peer)
        ).wait_recv()
    for share in shares:
        share.wait_send()
    for half in range(cores):
        for place in range(count):
            work[place * per:(place + 1) * per, half * block:(half + 1) * block] = gathered[half, place]

    reflect(vectors_ref, weights, work, inner, taus)

    step_cols = min(block, 512)
    halves[0] = jnp.zeros_like(halves[0])
    for start in range(0, block, step_cols):
        cols = slice(start, start + step_cols)
        own = weights[:, pl.ds(pl.multiple_of(core * block + start, 128), step_cols)] * scale_ref[:, cols]
        halves[0] += lax.dot_general(
            own, library_ref[:, cols].astype(jnp.float32), (((1,), (1,)), ((), ())),
            precision=HIGH, preferred_element_type=jnp.float32,
        )
    shares = []
    for step in range(1, cores):
        peer = lax.rem(core + step, cores)
        shares.append(
            remote(halves.at[0], halves.at[step], half_sems.at[0, step], half_sems.at[1, step], (me, peer))
        )
        shares[-1].start()
    for share in shares:
        share.wait()
    summed = halves[0]
    for step in range(1, cores):
        summed = summed + halves[step]
    for start in range(0, block, step_cols):
        cols = slice(start, start + step_cols)
        chunk = jnp.dot(
            summed, library_ref[:, cols].astype(jnp.float32), precision=HIGH, preferred_element_type=jnp.float32
        )
        for place in range(count):
            part_two[place, :, cols] = chunk[place * per:(place + 1) * per, :]
    sum_rows(count, part_two, landed_two, gathered_two, [row_sems_two.at[k] for k in range(4)])
    for place in range(count):
        mixed_ref[place * per:(place + 1) * per, :] = gathered_two[place] * scale_ref[...]


def panel_chain(part, library, scale, count, cores):
    width, block = part.shape
    rows_dev = library.shape[0]
    per = width // count
    size = block * cores
    real = jnp.float32
    slices = pltpu.VMEM((count, per, block), real)
    return pl.pallas_call(
        functools.partial(panel_kernel, count, cores),
        out_shape=(jax.ShapeDtypeStruct((width, size), real), jax.ShapeDtypeStruct((width, block), real)),
        in_specs=[pl.BlockSpec(memory_space=pltpu.VMEM)] * 3,
        out_specs=(pl.BlockSpec(memory_space=pltpu.VMEM),) * 2,
        scratch_shapes=[
            slices, slices, pltpu.VMEM((cores, count, per, block), real),
            slices, slices, slices, pltpu.VMEM((cores, width, rows_dev), real),
            pltpu.VMEM((width, size), real), pltpu.VMEM((width, size), real),
            pltpu.VMEM((width, width), real), pltpu.VMEM((width, 128), real),
            pltpu.SemaphoreType.DMA((4, count)), pltpu.SemaphoreType.DMA((4, count)),
            pltpu.SemaphoreType.DMA((2, cores)), pltpu.SemaphoreType.DMA((2, cores)),
        ],
        compiler_params=pltpu.CompilerParams(
            vmem_limit_bytes=32 << 20, collective_id=0, has_side_effects=True
        ),
        cost_estimate=pl.CostEstimate(flops=20_000_000_000, bytes_accessed=200_000_000, transcendentals=0),
    )(part, library, scale)


X_ITEMS = (
    ("own", 0, 0), ("own", 1, 2), ("own", 1, 0), ("fwd", 0, 0), ("own", 0, 1), ("fwd", 0, 1),
    ("own", 1, 3), ("own", 1, 1), ("fwd", 0, 2), ("own", 0, 2), ("fwd", 0, 3), ("own", 0, 3),
)
Y_ITEMS = (
    ("own", 0, 0), ("own", 0, 1), ("own", 1, 0), ("fwd", 1, 0), ("own", 1, 2), ("fwd", 1, 2),
    ("own", 0, 3), ("own", 0, 2), ("fwd", 1, 1), ("own", 1, 1), ("fwd", 1, 3), ("own", 1, 3),
)
ITEMS = {1: X_ITEMS, 2: Y_ITEMS}
STEPS = ((0, 0), (1, 0), (0, 1), (1, 2), (0, 2), (1, 1), (0, 3), (1, 3))
READY = (4, 4, 6, 6, 10, 10, 12, 12)
TOP = 2.0 ** 15.5
LEAST = 2.0 ** -125


def flip(place, mask):
    low, high = lax.rem(place, 2), place // 2
    low = 1 - low if mask & 1 else low
    high = 1 - high if mask & 2 else high
    return high * 2 + low


def encode(value, target, unit):
    level = value * (TOP / unit)
    square = level * level
    fourth = square * square
    eighth = fourth * fourth
    target[...] = jnp.where(level < 0.0, -eighth, eighth).astype(jnp.bfloat16)


def decode(source, unit):
    code = source[...].astype(jnp.float32)
    second = lax.rsqrt(lax.rsqrt(jnp.maximum(jnp.abs(code), LEAST)))
    value = second * lax.rsqrt(second) * (unit * (1.0 / TOP))
    return jnp.where(code < 0.0, -value, value)


def reflect_group(base, work, vectors, taus, inner):
    width, size = work.shape
    lane = lax.broadcasted_iota(jnp.int32, (1, 128), 1)

    def one_step(step, carry):
        place = base + step
        row = work[pl.ds(place, 1), :]
        head, tail = jnp.where(lane >= place, row[:, 0:128], 0.0), row[:, 128:size]
        near = work[base:base + 8, 0:128]
        rest = work[base:base + 8, 128:size]
        square = jnp.sum(head * head, axis=1, keepdims=True) + jnp.sum(tail * tail, axis=1, keepdims=True)
        pivot = jnp.sum(jnp.where(lane == place, head, 0.0), axis=1, keepdims=True)
        project = jnp.sum(near * head, axis=1, keepdims=True) + jnp.sum(rest * tail, axis=1, keepdims=True)
        across = jnp.sum(jnp.where(lane == place, near, 0.0), axis=1, keepdims=True)
        length = jnp.sqrt(square)
        signed = jnp.where(pivot >= 0.0, length, -length)
        tau = 1.0 / (length * (length + jnp.abs(pivot)))
        weight = tau * (project + signed * across)
        head = head + jnp.where(lane == place, signed, 0.0)
        work[base:base + 8, 0:128] = near - weight * head
        work[base:base + 8, 128:size] = rest - weight * tail
        vectors[pl.ds(place, 1), :] = jnp.concatenate([head, tail], axis=1)
        taus[pl.ds(place, 1), :] = jnp.broadcast_to(tau, (1, 128))
        return carry

    lax.fori_loop(0, 8, one_step, 0)
    if base + 8 == width:
        return

    def couple(step, carry):
        column = jnp.sum(vectors[base:base + 8, :] * vectors[pl.ds(base + step, 1), :], axis=1, keepdims=True)
        inner[step] = jnp.broadcast_to(column, (8, 128))
        return carry

    lax.fori_loop(0, 8, couple, 0, unroll=True)

    def trail(group, carry):
        rows = pl.ds(pl.multiple_of(group * 8, 8), 8)
        rest = work[rows, :]
        dots = [jnp.sum(rest * vectors[base + k:base + k + 1, :], axis=1, keepdims=True) for k in range(8)]
        weights = []
        for k in range(8):
            value = dots[k]
            for i in range(k):
                value = value - weights[i] * inner[k, i:i + 1, :]
            weights.append(value * taus[base + k:base + k + 1, :])
        for k in range(8):
            rest = rest - weights[k][:, 0:1] * vectors[base + k:base + k + 1, :]
        work[rows, :] = rest
        return carry

    lax.fori_loop(base // 8 + 1, width // 8, trail, 0, unroll=True)


def triangle(vectors, taus, factor_ref):
    width = vectors.shape[0]
    rows = vectors[...]
    gram = lax.dot_general(rows, rows, (((1,), (1,)), ((), ())), precision=HIGH, preferred_element_type=jnp.float32)
    across = lax.broadcasted_iota(jnp.int32, (width, width), 1)
    down = lax.broadcasted_iota(jnp.int32, (width, width), 0)
    factor = jnp.where(across == down, taus[:, 0:1], 0.0)
    span = 1
    while span < width:
        pick = (down // span + 1 == across // span) & (across // (2 * span) == down // (2 * span))
        middle = jnp.dot(factor, jnp.where(pick, gram, 0.0), precision=HIGH, preferred_element_type=jnp.float32)
        factor = factor - jnp.dot(middle, factor, precision=HIGH, preferred_element_type=jnp.float32)
        span *= 2
    factor_ref[...] = factor


def halves_of(value):
    high = value.astype(jnp.bfloat16)
    return high, (value - high.astype(jnp.float32)).astype(jnp.bfloat16)


def whole_kernel(
    total, library_ref, scale_ref, updated_ref, own_ref,
    whole, left, prod, code_a, code_c, land_a, land_b, land_c,
    head_raw, heads, part, landed, summed, gathered, crossed, work, vectors, taus, inner_dots, factor,
    sample_dots, stacked, thin, bounds, first_part, first_landed, first_sum, first_near,
    plane_send, plane_recv, own_sem, left_send, left_recv, z_send, z_recv,
    head_send, head_recv, sum_send, sum_recv, core_send, core_recv, bound_send, bound_recv, first_send, first_recv,
):
    me, core = lax.axis_index("rows"), lax.axis_index("grid")
    far, near = left.shape[0], 4
    place, level = lax.rem(me, near), me // near
    samples = library_ref.shape[0]
    size = left.shape[1]
    block = library_ref.shape[1]
    width = work.shape[0]
    chunk = size // 2
    buddy = level + 1 - 2 * lax.rem(level, 2)
    base = 2 * (1 - level // 2)
    inner = lax.rem(level + 1, far) // 2 == 1
    outer = lax.rem(level + 1, far) // 2 == 0
    other = (me, 1 - core)
    full = jnp.float32

    def chip(mask):
        return (level * near + flip(place, mask), core)

    def floor(which):
        return (which * near + place, core)

    def beside(step):
        return lax.rem(level + step, far)

    barrier = pltpu.get_barrier_semaphore()
    for target in (chip(1), chip(2), chip(3), floor(beside(1)), floor(beside(2)), floor(beside(3)), other):
        pl.semaphore_signal(barrier, inc=1, device_id=target, device_id_type=MESH)
    pl.semaphore_wait(barrier, 7)

    def columns(zz, group):
        return pl.ds(pl.multiple_of((zz * near + group) * size, size), size)

    def spot(zz, r, source):
        return whole.at[zz * near + r, pl.ds(source * samples, samples)]

    def item(mask, k):
        kind, zz, r = ITEMS[mask][k]
        if kind == "own":
            source = library_ref.at[:, columns(zz, flip(place, r ^ mask))]
            target = spot(zz, r, mask)
        else:
            source = spot(zz, r ^ mask, 3 ^ mask)
            target = spot(zz, r, 3)
        return remote(source, target, plane_send.at[mask - 1, k], plane_recv.at[mask - 1, k], chip(mask))

    seen, sent = set(), []

    def arrive(mask, k):
        if (mask, k) not in seen:
            seen.add((mask, k))
            item(mask, k).wait_recv()

    def send(mask, k):
        kind, zz, r = ITEMS[mask][k]
        if kind == "fwd":
            arrive(3 ^ mask, ITEMS[3 ^ mask].index(("own", zz, r ^ mask)))
        item(mask, k).start()
        sent.append((mask, k))

    def both(action, k):
        action(1, k)
        action(2, k)

    copies = []
    for zz in range(2):
        for r in range(4):
            copies.append(pltpu.make_async_copy(
                library_ref.at[:, columns(zz, flip(place, r))], spot(zz, r, 0), own_sem.at[zz * near + r]))
    head_copy = pltpu.make_async_copy(library_ref.at[:, 0:128], head_raw, own_sem.at[8])
    head_copy.start()
    copies[0].start()
    copies[near].start()
    for k in range(3):
        both(send, k)
    for index, copy in enumerate(copies):
        if index % near:
            copy.start()

    placed = set()

    def landed_own(zz, r):
        if (zz, r) not in placed:
            placed.add((zz, r))
            copies[zz * near + r].wait()

    def head_over():
        return remote(heads, heads, head_send.at[0], head_recv.at[0], other)

    head_copy.wait()

    @pl.when(core == 0)
    def _():
        heads[...] = head_raw[...].T[0:width, :]
        head_over().start()

    def piece(zz, source, half):
        target = left.at[2 * half + zz, :, pl.ds(source * samples, samples)]
        index = zz * near + source
        return remote(target, target, left_send.at[index], left_recv.at[index], other)

    def turn(zz, source):
        left[2 * core + zz, :, source * samples:(source + 1) * samples] = (
            whole[zz * near, source * samples:(source + 1) * samples, :].T
        )
        piece(zz, source, core).start()

    for zz in range(2):
        landed_own(zz, 0)
        turn(zz, 0)
    for zz, r in STEPS:
        landed_own(zz, r)

    @pl.when(core == 1)
    def _():
        head_over().wait_recv()

    def first_far(step):
        peer = beside(step)
        return remote(first_part.at[peer], first_landed.at[step], first_send.at[0, step], first_recv.at[0, step],
                      floor(peer))

    def first_close(mask):
        return remote(first_sum.at[mask], first_near.at[mask], first_send.at[1, mask], first_recv.at[1, mask],
                      chip(mask))

    for zz in range(2):
        for r in range(near):
            value = jnp.dot(heads[...], whole[zz * near + r, 0:samples, :], preferred_element_type=full)
            first_part[2 * zz, r] = value[:, 0:chunk]
            first_part[2 * zz + 1, r] = value[:, chunk:size]
    for step in (2, 1, 3):
        first_far(step).start()

    def squares(index, peak):
        value = whole[index, 0:samples, :].astype(full)
        return jnp.maximum(peak, jnp.sum(value * value, axis=0, keepdims=True))

    def keep(index, value):
        bounds[index] = jnp.broadcast_to(value, (8, 128))

    def bound(index):
        if index == 0:
            source, target, place_of = 0, 1, other
        elif index < near:
            source, target, place_of = 2, 2 + index, chip(index)
        else:
            source, target, place_of = 6, 6 + index - 3, floor(beside(index - 3))
        return remote(bounds.at[source], bounds.at[target], bound_send.at[index], bound_recv.at[index], place_of)

    def unit_of(which):
        slot = 6 + lax.rem(level - which + far, far)
        return bounds[slot][0:1, 0:1]

    keep(0, jnp.max(
        lax.fori_loop(0, 2 * near, squares, jnp.zeros((1, size), full)), axis=1, keepdims=True))
    bound(0).start()
    both(arrive, 0)
    turn(0, 1)
    turn(0, 2)
    bound(0).wait_recv()
    keep(2, jnp.maximum(bounds[0], bounds[1])[0:1, 0:1])
    for mask in (3, 1, 2):
        bound(mask).start()
    both(arrive, 1)
    both(send, 3)
    both(arrive, 2)
    value = first_part[level]
    for step in range(1, far):
        first_far(step).wait_recv()
        value = value + first_landed[step]
    first_sum[...] = value
    for mask in (3, 1, 2):
        first_close(mask).start()
    both(send, 4)
    for mask in (1, 2, 3):
        bound(mask).wait_recv()
    keep(6, jnp.maximum(bounds[2] + bounds[3] + bounds[4] + bounds[5], 1e-30)[0:1, 0:1])
    for step in (2, 1, 3):
        bound(3 + step).start()
    turn(1, 1)
    turn(1, 2)

    both(arrive, 3)
    turn(0, 3)
    turn(1, 3)
    for step in range(1, far):
        bound(3 + step).wait_recv()
    unit_own = unit_of(level)
    unit_pair = unit_own + unit_of(buddy)
    unit_buddy = unit_of(buddy)
    unit_far = unit_of(base) + unit_of(base + 1)

    def scatter(which, step):
        peer = beside(step)
        return remote(part.at[which, peer], landed.at[which, step], sum_send.at[which, 0, step],
                      sum_recv.at[which, 0, step], floor(peer))

    def spread(which, step, arriving=False):
        spot_of = summed.at[which, beside(far - step)] if arriving else summed.at[which, level]
        return remote(spot_of, spot_of, sum_send.at[which, 1, step], sum_recv.at[which, 1, step], floor(beside(step)))

    def fan(which, mask):
        return remote(summed.at[which], gathered.at[which, mask], sum_send.at[which, 2, mask],
                      sum_recv.at[which, 2, mask], chip(mask))

    def begin_sum(which):
        for step in (2, 1, 3):
            scatter(which, step).start()

    def add_up(which):
        value = part[which, level]
        for step in range(1, far):
            scatter(which, step).wait_recv()
            value = value + landed[which, step]
        summed[which, level] = value
        for step in (2, 1, 3):
            spread(which, step).start()

    def fan_out(which):
        for step in range(1, far):
            spread(which, step, True).wait_recv()
        for mask in (3, 1, 2):
            fan(which, mask).start()
        gathered[which, 0] = summed[which]

    def fan_in(which):
        for mask in range(1, near):
            fan(which, mask).wait_recv()

    def end_sum(which):
        for step in range(1, far):
            if which:
                scatter(which, step).wait_send()
            else:
                first_far(step).wait_send()
            spread(which, step).wait_send()
        for mask in range(1, near):
            fan(which, mask).wait_send()

    value = first_sum[0]
    for mask in range(1, near):
        first_close(mask).wait_recv()
        value = value + first_near[mask]
    summed[0, level] = value
    for step in (2, 1, 3):
        spread(0, step).start()

    def share(t, kind, which=0):
        if kind == "a":
            return remote(code_a.at[t], land_a.at[t], z_send.at[t, 0], z_recv.at[t, 0], floor(buddy))
        if kind == "c":
            return remote(code_c.at[t, which], land_c.at[t, which], z_send.at[t, 1 + which],
                          z_recv.at[t, 1 + which], floor(buddy))
        return remote(code_c.at[t, which], land_b.at[t], z_send.at[t, 1 + which], z_recv.at[t, 3],
                      floor(base + which))

    def combine(t):
        @pl.when(inner)
        def _():
            def one(which, carry):
                share(t, "c", which).wait_recv()
                encode(prod[t, base + which] + decode(land_c.at[t, which], unit_buddy), code_c.at[t, which], unit_pair)
                share(t, "b", which).start()
                return carry

            lax.fori_loop(0, 2, one, 0)

    def multiply(t):
        zz, r = STEPS[t]
        for k in range(READY[t]):
            both(arrive, k)
        landed_own(zz, r)

        def product(target):
            prod[t, target] = jnp.dot(left[target], whole[zz * near + r], preferred_element_type=full)

        def one(which, carry):
            product(base + which)

            @pl.when(outer)
            def _():
                encode(prod[t, base + which], code_c.at[t, which], unit_own)
                share(t, "c", which).start()

            return carry

        lax.fori_loop(0, 2, one, 0)
        product(buddy)
        encode(prod[t, buddy], code_a.at[t], unit_own)
        product(level)

    def send_a(t):
        share(t, "a").start()

    for zz in range(2):
        for source in range(4):
            piece(zz, source, 1 - core).wait_recv()
    multiply(0)
    multiply(1)
    fan_out(0)
    both(send, 5)
    both(send, 6)
    send_a(0)
    send_a(1)
    combine(0)
    fan_in(0)

    def over(which):
        if which == 0:
            return remote(gathered.at[0], crossed, core_send.at[0], core_recv.at[0], other)
        return remote(sample_dots.at[0], sample_dots.at[1], core_send.at[1], core_recv.at[1], other)

    over(0).start()
    over(0).wait_recv()

    first = jnp.broadcast_to(scale_ref[:, 0:128], (8, 128)).T[0:width, 0:1] * (1.0 / total)
    for mask in range(near):
        for k in range(4):
            column = ((k // 2) * near + flip(place, mask)) * size + (k % 2) * chunk
            for side, half in ((0, core), (1, 1 - core)):
                cols = pl.ds(pl.multiple_of(half * block + column, chunk), chunk)
                value = gathered[0, mask, k] if side == 0 else crossed[mask, k]
                work[:, cols] = value * (first * scale_ref[:, cols])

    for group in range(width // 8):
        reflect_group(8 * group, work, vectors, taus, inner_dots)
        if group == 0:
            both(send, 7)
            multiply(2)
        if group == 1:
            combine(1)
            multiply(3)
            send_a(2)
            send_a(3)
        if group == 2:
            both(send, 8)
            both(send, 9)
        if group == 3:
            combine(2)
        if group == 4:
            both(send, 10)
        if group == 5:
            combine(3)

    def dots(zz, r):
        cols = columns(zz, flip(place, r))
        there = pl.ds(pl.multiple_of(core * block + (zz * near + flip(place, r)) * size, size), size)
        value = vectors[:, there] * scale_ref[:, there]
        high, low = halves_of(value)
        thin[zz * near + r] = jnp.concatenate([high, low], axis=0).T

    for zz in range(2):
        for r in range(4):
            dots(zz, r)
    value = jnp.dot(whole[0, 0:samples, :], thin[0], preferred_element_type=full)
    for index in range(1, 2 * near):
        value = value + jnp.dot(whole[index, 0:samples, :], thin[index], preferred_element_type=full)
    value = value.T
    sample_dots[0] = value[0:width, :] + value[width:2 * width, :]
    over(1).start()
    triangle(vectors, taus, factor)
    multiply(4)
    over(1).wait_recv()
    value = lax.dot_general(
        factor[...], sample_dots[0] + sample_dots[1], (((0,), (0,)), ((), ())), precision=HIGH,
        preferred_element_type=full)
    high, low = halves_of(value)
    stacked[0:width, 0:samples] = high
    stacked[width:2 * width, 0:samples] = low

    def stack(mask):
        return remote(stacked.at[:, 0:samples], stacked.at[:, mask * samples:(mask + 1) * samples],
                      sum_send.at[2, 2, mask], sum_recv.at[2, 2, mask], chip(mask))

    for mask in (3, 1, 2):
        stack(mask).start()
    both(send, 11)
    multiply(5)
    combine(4)
    for mask in (1, 2, 3):
        stack(mask).wait_recv()
    for zz in range(2):
        value = jnp.dot(stacked[...], whole[zz * near], preferred_element_type=full)
        value = value[0:width, :] + value[width:2 * width, :]
        part[1, 2 * zz] = value[:, 0:chunk]
        part[1, 2 * zz + 1] = value[:, chunk:size]
    begin_sum(1)
    send_a(4)
    combine(5)
    add_up(1)
    multiply(6)
    fan_out(1)
    multiply(7)
    send_a(5)
    send_a(6)
    send_a(7)
    combine(6)

    mine = pl.ds(pl.multiple_of(me * size, size), size)
    ours = vectors[:, mine]
    own_ref[...] = ours
    high, low = halves_of(ours)
    thin_rows = jnp.concatenate([high, high, low, low], axis=0).T
    row_scale = jnp.broadcast_to(scale_ref[:, mine], (8, size)).T[:, 0:1] * (1.0 / total)
    combine(7)
    fan_in(1)

    for t, (zz, r) in enumerate(STEPS):
        cols = columns(zz, flip(place, r))
        there = pl.ds(pl.multiple_of(core * block + (zz * near + flip(place, r)) * size, size), size)
        scale = scale_ref[:, there]
        value = jnp.concatenate([gathered[1, r, 2 * zz], gathered[1, r, 2 * zz + 1]], axis=1)
        high, low = halves_of(value * (scale * (1.0 / total)))
        change = jnp.dot(thin_rows, jnp.concatenate([high, low, high, low], axis=0), preferred_element_type=full)
        share(t, "a").wait_recv()
        share(t, "b").wait_recv()
        value = prod[t, level] + decode(land_a.at[t], unit_buddy) + decode(land_b.at[t], unit_far)
        updated_ref[:, cols] = value * (row_scale * scale) - change

    for mask, k in sent:
        item(mask, k).wait_send()
    for zz in range(2):
        for source in range(4):
            piece(zz, source, core).wait_send()
    for t in range(len(STEPS)):
        share(t, "a").wait_send()
        for which in range(2):
            share(t, "c", which).wait_send()
    end_sum(0)
    end_sum(1)
    for mask in range(1, near):
        stack(mask).wait_send()
    for index in range(7):
        bound(index).wait_send()
    over(0).wait_send()
    over(1).wait_send()

    for mask in range(1, near):
        first_close(mask).wait_send()

    @pl.when(core == 0)
    def _():
        head_over().wait_send()


def whole_update(library, col_scale, far):
    samples, block = library.shape
    near, cores = 4, 2
    columns = block * cores
    size = columns // (near * far)
    steps = block // size
    half, full = jnp.bfloat16, jnp.float32
    coded = (size, size)
    dma = pltpu.SemaphoreType.DMA
    vmem = pl.BlockSpec(memory_space=pltpu.VMEM)
    small = (PANEL, size // 2)
    updated, own = pl.pallas_call(
        functools.partial(whole_kernel, samples * near * far),
        out_shape=(jax.ShapeDtypeStruct((size, block), full), jax.ShapeDtypeStruct((PANEL, size), full)),
        in_specs=[pl.BlockSpec(memory_space=pl.ANY), vmem],
        out_specs=(vmem, vmem),
        scratch_shapes=[
            pltpu.VMEM((steps, near * samples, size), half), pltpu.VMEM((far, size, near * samples), half),
            pltpu.VMEM((steps, far, size, size), full),
            pltpu.VMEM((steps,) + coded, half), pltpu.VMEM((steps, 2) + coded, half),
            pltpu.VMEM((steps,) + coded, half), pltpu.VMEM((steps,) + coded, half),
            pltpu.VMEM((steps, 2) + coded, half),
            pltpu.VMEM((samples, 128), half), pltpu.VMEM((PANEL, samples), half),
            pltpu.VMEM((2, far) + small, full), pltpu.VMEM((2, far) + small, full),
            pltpu.VMEM((2, far) + small, full), pltpu.VMEM((2, near, far) + small, full),
            pltpu.VMEM((near, far) + small, full),
            pltpu.VMEM((PANEL, columns), full), pltpu.VMEM((PANEL, columns), full),
            pltpu.VMEM((PANEL, 128), full), pltpu.VMEM((8, 8, 128), full), pltpu.VMEM((PANEL, PANEL), full),
            pltpu.VMEM((2, PANEL, samples), full), pltpu.VMEM((2 * PANEL, near * samples), half),
            pltpu.VMEM((steps, size, 2 * PANEL), half), pltpu.VMEM((10, 8, 128), full),
            pltpu.VMEM((far, near) + small, full), pltpu.VMEM((far, near) + small, full),
            pltpu.VMEM((near,) + small, full), pltpu.VMEM((near,) + small, full),
            dma((2, 12)), dma((2, 12)), dma((9,)), dma((8,)), dma((8,)), dma((steps, 3)), dma((steps, 4)),
            dma((4,)), dma((4,)), dma((3, 3, 4)), dma((3, 3, 4)), dma((2,)), dma((2,)), dma((7,)), dma((7,)), dma((2, 4)), dma((2, 4)),
        ],
        compiler_params=pltpu.CompilerParams(
            vmem_limit_bytes=44 << 20, collective_id=1, has_side_effects=True
        ),
        cost_estimate=pl.CostEstimate(flops=12_000_000_000, bytes_accessed=10_000_000, transcendentals=0),
    )(library, col_scale)
    return updated, own.T


def per_device(library, col_scale):
    rows_dev, col_block = library.shape
    count_rows = lax.axis_size("rows")
    count_grid = lax.axis_size("grid")
    columns = col_block * count_grid
    row_block = columns // count_rows
    total = rows_dev * count_rows
    near = 1
    while near * near < count_rows:
        near *= 2
    far = count_rows // near
    if count_rows == 16 and count_grid == 2 and row_block % 256 == 0 and rows_dev % 128 == 0:
        return whole_update(library, col_scale[None, :], 4)
    grid_place = lax.axis_index("grid")
    rows_place = lax.axis_index("rows")
    near_groups = [[f * near + n for n in range(near)] for f in range(far)]
    far_groups = [[f * near + n for f in range(far)] for n in range(near)]
    own_scale = lax.dynamic_slice_in_dim(col_scale, grid_place * col_block, col_block)

    head = lax.all_gather(library[:, :PANEL], "grid", axis=0)[0]
    panel_part = lax.dot_general(
        head, library, (((0,), (0,)), ((), ())), preferred_element_type=jnp.float32
    )
    panel_part = panel_part * (col_scale[:PANEL, None] * own_scale[None, :] / total)
    vectors, mixed = panel_chain(panel_part, library, own_scale[None, :], count_rows, count_grid)
    mixed = mixed / total

    whole = lax.all_gather(library, "rows", axis=0, tiled=True, axis_index_groups=near_groups)
    whole, vectors, mixed = lax.optimization_barrier((whole, vectors, mixed))
    place = rows_place % near
    blocks = whole.T.reshape(far // count_grid, near, row_block, near * rows_dev)
    left = lax.dynamic_index_in_dim(blocks, place, 1, keepdims=False)
    left = left.reshape(far // count_grid * row_block, near * rows_dev)
    left = lax.all_gather(left, "grid", axis=0, tiled=True)
    product = lax.dot_general(
        left, whole, (((1,), (0,)), ((), ())), preferred_element_type=jnp.float32
    )
    gram = lax.psum_scatter(
        product, "rows", scatter_dimension=0, tiled=True, axis_index_groups=far_groups
    )
    row_scale = lax.dynamic_slice_in_dim(col_scale, rows_place * row_block, row_block)

    own_vectors = lax.dynamic_slice_in_dim(vectors, rows_place * row_block, row_block, 1).T
    gram = gram * (row_scale[:, None] * own_scale[None, :] / total)
    updated = gram - jnp.dot(own_vectors, mixed, precision=HIGH)
    return (updated, own_vectors)


def solution(mesh):
    return jax.shard_map(
        per_device,
        mesh=mesh,
        in_specs=(P("rows", "grid"), P()),
        out_specs=(P("rows", "grid"), P("rows", None)),
        check_vma=False,
    )
```

```python
import functools

import jax
import jax.numpy as jnp
from jax import lax
from jax.experimental import pallas as pl
from jax.experimental.pallas import tpu as pltpu
from jax.sharding import PartitionSpec as P

PANEL = 64
HIGH = lax.Precision.HIGHEST
MESH = pl.DeviceIdType.MESH


def reflect(vectors_ref, weights_ref, work, inner, taus):
    width, size = work.shape
    lane = lax.broadcasted_iota(jnp.int32, (1, size), 1)
    for base in range(0, width, 8):

        def one_step(step, carry, base=base):
            place = base + step
            row = work[pl.ds(place, 1), :]
            row = jnp.where(lane >= place, row, 0.0)
            pivot = jnp.sum(jnp.where(lane == place, row, 0.0), axis=1, keepdims=True)
            length = jnp.sqrt(jnp.sum(row * row, axis=1, keepdims=True))
            signed = jnp.where(pivot >= 0.0, length, -length)
            vector = row + jnp.where(lane == place, signed, 0.0)
            tau = 1.0 / (length * (length + jnp.abs(pivot)))
            rest = work[base:, :]
            project = jnp.sum(rest * vector, axis=1, keepdims=True)
            work[base:, :] = rest - (tau * project) * vector
            vectors_ref[pl.ds(place, 1), :] = vector
            taus[pl.ds(place, 1), :] = jnp.broadcast_to(tau, (1, 128))
            return carry

        lax.fori_loop(0, 8, one_step, 0)
    vectors = vectors_ref[...]
    inner[...] = lax.dot_general(
        vectors, vectors, (((1,), (1,)), ((), ())), precision=HIGH, preferred_element_type=jnp.float32
    )
    across = lax.broadcasted_iota(jnp.int32, (width, width), 1)
    down = lax.broadcasted_iota(jnp.int32, (width, 1), 0)

    def factor_step(place, factor):
        tau = taus[pl.ds(place, 1), 0:1]
        coupling = jnp.where(across < place, inner[pl.ds(place, 1), :] * factor, 0.0)
        column = -tau * jnp.sum(coupling, axis=1, keepdims=True)
        column = column + jnp.where(down == place, tau, 0.0)
        return jnp.where(across == place, column, factor)

    factor = lax.fori_loop(0, width, factor_step, jnp.zeros((width, width), jnp.float32))
    weights_ref[...] = lax.dot_general(
        factor, vectors, (((0,), (0,)), ((), ())), precision=HIGH, preferred_element_type=jnp.float32
    )


def remote(source, target, send, recv, place):
    return pltpu.make_async_remote_copy(
        src_ref=source, dst_ref=target, send_sem=send, recv_sem=recv,
        device_id=place, device_id_type=pl.DeviceIdType.MESH,
    )


def sum_rows(count, part, landed, out, sems):
    me, core = lax.axis_index("rows"), lax.axis_index("grid")
    send, recv, send_back, recv_back = sems

    def scatter(step):
        peer = lax.rem(me + step, count)
        return remote(part.at[peer], landed.at[step], send.at[step], recv.at[step], (peer, core))

    def spread(step):
        peer = lax.rem(me + step, count)
        return remote(out.at[me], out.at[me], send_back.at[step], recv_back.at[step], (peer, core))

    def arrival(step):
        peer = lax.rem(me + count - step, count)
        return remote(out.at[peer], out.at[peer], send_back.at[step], recv_back.at[step], (peer, core))

    def loop(action):
        def body(step, carry):
            action(step)
            return carry
        lax.fori_loop(1, count, body, 0)

    loop(lambda step: scatter(step).start())
    loop(lambda step: scatter(step).wait_recv())
    total = part[me]
    for step in range(1, count):
        total = total + landed[step]
    out[me] = total
    loop(lambda step: spread(step).start())
    loop(lambda step: arrival(step).wait_recv())
    loop(lambda step: scatter(step).wait_send())
    loop(lambda step: spread(step).wait_send())


def panel_kernel(
    count, cores, part_ref, library_ref, scale_ref, vectors_ref, mixed_ref,
    part, landed, gathered, part_two, landed_two, gathered_two, halves,
    weights, work, inner, taus, row_sems, row_sems_two, core_sems, half_sems,
):
    me, core = lax.axis_index("rows"), lax.axis_index("grid")
    width, block = part_ref.shape
    per = width // count
    barrier = pltpu.get_barrier_semaphore()

    def greet(step, carry):
        pl.semaphore_signal(
            barrier, inc=1, device_id=(lax.rem(me + step, count), core), device_id_type=pl.DeviceIdType.MESH
        )
        return carry

    lax.fori_loop(1, count, greet, 0)
    for step in range(1, cores):
        pl.semaphore_signal(
            barrier, inc=1, device_id=(me, lax.rem(core + step, cores)), device_id_type=pl.DeviceIdType.MESH
        )
    for place in range(count):
        part[place] = part_ref[place * per:(place + 1) * per, :]
    pl.semaphore_wait(barrier, count + cores - 2)

    sum_rows(count, part, landed, gathered.at[core], [row_sems.at[k] for k in range(4)])
    shares = []
    for step in range(1, cores):
        peer = lax.rem(core + step, cores)
        shares.append(
            remote(gathered.at[core], gathered.at[core], core_sems.at[0, step], core_sems.at[1, step], (me, peer))
        )
        shares[-1].start()
    for step in range(1, cores):
        peer = lax.rem(core + cores - step, cores)
        remote(
            gathered.at[peer], gathered.at[peer], core_sems.at[0, step], core_sems.at[1, step], (me, peer)
        ).wait_recv()
    for share in shares:
        share.wait_send()
    for half in range(cores):
        for place in range(count):
            work[place * per:(place + 1) * per, half * block:(half + 1) * block] = gathered[half, place]

    reflect(vectors_ref, weights, work, inner, taus)

    step_cols = min(block, 512)
    halves[0] = jnp.zeros_like(halves[0])
    for start in range(0, block, step_cols):
        cols = slice(start, start + step_cols)
        own = weights[:, pl.ds(pl.multiple_of(core * block + start, 128), step_cols)] * scale_ref[:, cols]
        halves[0] += lax.dot_general(
            own, library_ref[:, cols].astype(jnp.float32), (((1,), (1,)), ((), ())),
            precision=HIGH, preferred_element_type=jnp.float32,
        )
    shares = []
    for step in range(1, cores):
        peer = lax.rem(core + step, cores)
        shares.append(
            remote(halves.at[0], halves.at[step], half_sems.at[0, step], half_sems.at[1, step], (me, peer))
        )
        shares[-1].start()
    for share in shares:
        share.wait()
    summed = halves[0]
    for step in range(1, cores):
        summed = summed + halves[step]
    for start in range(0, block, step_cols):
        cols = slice(start, start + step_cols)
        chunk = jnp.dot(
            summed, library_ref[:, cols].astype(jnp.float32), precision=HIGH, preferred_element_type=jnp.float32
        )
        for place in range(count):
            part_two[place, :, cols] = chunk[place * per:(place + 1) * per, :]
    sum_rows(count, part_two, landed_two, gathered_two, [row_sems_two.at[k] for k in range(4)])
    for place in range(count):
        mixed_ref[place * per:(place + 1) * per, :] = gathered_two[place] * scale_ref[...]


def panel_chain(part, library, scale, count, cores):
    width, block = part.shape
    rows_dev = library.shape[0]
    per = width // count
    size = block * cores
    real = jnp.float32
    slices = pltpu.VMEM((count, per, block), real)
    return pl.pallas_call(
        functools.partial(panel_kernel, count, cores),
        out_shape=(jax.ShapeDtypeStruct((width, size), real), jax.ShapeDtypeStruct((width, block), real)),
        in_specs=[pl.BlockSpec(memory_space=pltpu.VMEM)] * 3,
        out_specs=(pl.BlockSpec(memory_space=pltpu.VMEM),) * 2,
        scratch_shapes=[
            slices, slices, pltpu.VMEM((cores, count, per, block), real),
            slices, slices, slices, pltpu.VMEM((cores, width, rows_dev), real),
            pltpu.VMEM((width, size), real), pltpu.VMEM((width, size), real),
            pltpu.VMEM((width, width), real), pltpu.VMEM((width, 128), real),
            pltpu.SemaphoreType.DMA((4, count)), pltpu.SemaphoreType.DMA((4, count)),
            pltpu.SemaphoreType.DMA((2, cores)), pltpu.SemaphoreType.DMA((2, cores)),
        ],
        compiler_params=pltpu.CompilerParams(
            vmem_limit_bytes=32 << 20, collective_id=0, has_side_effects=True
        ),
        cost_estimate=pl.CostEstimate(flops=20_000_000_000, bytes_accessed=200_000_000, transcendentals=0),
    )(part, library, scale)


X_ITEMS = (
    ("own", 0, 0), ("own", 1, 2), ("own", 1, 0), ("fwd", 0, 0), ("own", 0, 1), ("fwd", 0, 1),
    ("own", 1, 3), ("own", 1, 1), ("fwd", 0, 2), ("own", 0, 2), ("fwd", 0, 3), ("own", 0, 3),
)
Y_ITEMS = (
    ("own", 0, 0), ("own", 0, 1), ("own", 1, 0), ("fwd", 1, 0), ("own", 1, 2), ("fwd", 1, 2),
    ("own", 0, 3), ("own", 0, 2), ("fwd", 1, 1), ("own", 1, 1), ("fwd", 1, 3), ("own", 1, 3),
)
ITEMS = {1: X_ITEMS, 2: Y_ITEMS}
STEPS = ((0, 0), (1, 0), (0, 1), (1, 2), (0, 2), (1, 1), (0, 3), (1, 3))
READY = (4, 4, 6, 6, 10, 10, 12, 12)
TOP = 2.0 ** 15.5
LEAST = 2.0 ** -125


def flip(place, mask):
    low, high = lax.rem(place, 2), place // 2
    low = 1 - low if mask & 1 else low
    high = 1 - high if mask & 2 else high
    return high * 2 + low


def encode(value, target, unit):
    level = value * (TOP / unit)
    square = level * level
    fourth = square * square
    eighth = fourth * fourth
    target[...] = jnp.where(level < 0.0, -eighth, eighth).astype(jnp.bfloat16)


def decode(source, unit):
    code = source[...].astype(jnp.float32)
    second = lax.rsqrt(lax.rsqrt(jnp.maximum(jnp.abs(code), LEAST)))
    value = second * lax.rsqrt(second) * (unit * (1.0 / TOP))
    return jnp.where(code < 0.0, -value, value)


def reflect_group(base, work, vectors, taus, inner):
    width, size = work.shape
    lane = lax.broadcasted_iota(jnp.int32, (1, 128), 1)

    def one_step(step, carry):
        place = base + step
        row = work[pl.ds(place, 1), :]
        head, tail = jnp.where(lane >= place, row[:, 0:128], 0.0), row[:, 128:size]
        near = work[base:base + 8, 0:128]
        rest = work[base:base + 8, 128:size]
        square = jnp.sum(head * head, axis=1, keepdims=True) + jnp.sum(tail * tail, axis=1, keepdims=True)
        pivot = jnp.sum(jnp.where(lane == place, head, 0.0), axis=1, keepdims=True)
        project = jnp.sum(near * head, axis=1, keepdims=True) + jnp.sum(rest * tail, axis=1, keepdims=True)
        across = jnp.sum(jnp.where(lane == place, near, 0.0), axis=1, keepdims=True)
        length = jnp.sqrt(square)
        signed = jnp.where(pivot >= 0.0, length, -length)
        tau = 1.0 / (length * (length + jnp.abs(pivot)))
        weight = tau * (project + signed * across)
        head = head + jnp.where(lane == place, signed, 0.0)
        work[base:base + 8, 0:128] = near - weight * head
        work[base:base + 8, 128:size] = rest - weight * tail
        vectors[pl.ds(place, 1), :] = jnp.concatenate([head, tail], axis=1)
        taus[pl.ds(place, 1), :] = jnp.broadcast_to(tau, (1, 128))
        return carry

    lax.fori_loop(0, 8, one_step, 0)
    if base + 8 == width:
        return

    def couple(step, carry):
        column = jnp.sum(vectors[base:base + 8, :] * vectors[pl.ds(base + step, 1), :], axis=1, keepdims=True)
        inner[step] = jnp.broadcast_to(column, (8, 128))
        return carry

    lax.fori_loop(0, 8, couple, 0, unroll=True)

    def trail(group, carry):
        rows = pl.ds(pl.multiple_of(group * 8, 8), 8)
        rest = work[rows, :]
        dots = [jnp.sum(rest * vectors[base + k:base + k + 1, :], axis=1, keepdims=True) for k in range(8)]
        weights = []
        for k in range(8):
            value = dots[k]
            for i in range(k):
                value = value - weights[i] * inner[k, i:i + 1, :]
            weights.append(value * taus[base + k:base + k + 1, :])
        for k in range(8):
            rest = rest - weights[k][:, 0:1] * vectors[base + k:base + k + 1, :]
        work[rows, :] = rest
        return carry

    lax.fori_loop(base // 8 + 1, width // 8, trail, 0, unroll=True)


def triangle(vectors, taus, factor_ref):
    width = vectors.shape[0]
    rows = vectors[...]
    gram = lax.dot_general(rows, rows, (((1,), (1,)), ((), ())), precision=HIGH, preferred_element_type=jnp.float32)
    across = lax.broadcasted_iota(jnp.int32, (width, width), 1)
    down = lax.broadcasted_iota(jnp.int32, (width, width), 0)
    factor = jnp.where(across == down, taus[:, 0:1], 0.0)
    span = 1
    while span < width:
        pick = (down // span + 1 == across // span) & (across // (2 * span) == down // (2 * span))
        middle = jnp.dot(factor, jnp.where(pick, gram, 0.0), precision=HIGH, preferred_element_type=jnp.float32)
        factor = factor - jnp.dot(middle, factor, precision=HIGH, preferred_element_type=jnp.float32)
        span *= 2
    factor_ref[...] = factor


def halves_of(value):
    high = value.astype(jnp.bfloat16)
    return high, (value - high.astype(jnp.float32)).astype(jnp.bfloat16)


def whole_kernel(
    total, library_ref, scale_ref, updated_ref, own_ref,
    whole, left, prod, code_a, code_c, land_a, land_b, land_c,
    head_raw, heads, part, landed, summed, gathered, crossed, work, vectors, taus, inner_dots, factor,
    sample_dots, stacked, thin, bounds, first_part, first_landed, first_sum, first_near,
    plane_send, plane_recv, own_sem, left_send, left_recv, z_send, z_recv,
    head_send, head_recv, sum_send, sum_recv, core_send, core_recv, bound_send, bound_recv, first_send, first_recv,
):
    me, core = lax.axis_index("rows"), lax.axis_index("grid")
    far, near = left.shape[0], 4
    place, level = lax.rem(me, near), me // near
    samples = library_ref.shape[0]
    size = left.shape[1]
    block = library_ref.shape[1]
    width = work.shape[0]
    chunk = size // 2
    buddy = level + 1 - 2 * lax.rem(level, 2)
    base = 2 * (1 - level // 2)
    inner = lax.rem(level + 1, far) // 2 == 1
    outer = lax.rem(level + 1, far) // 2 == 0
    other = (me, 1 - core)
    full = jnp.float32

    def chip(mask):
        return (level * near + flip(place, mask), core)

    def floor(which):
        return (which * near + place, core)

    def beside(step):
        return lax.rem(level + step, far)

    barrier = pltpu.get_barrier_semaphore()
    for target in (chip(1), chip(2), chip(3), floor(beside(1)), floor(beside(2)), floor(beside(3)), other):
        pl.semaphore_signal(barrier, inc=1, device_id=target, device_id_type=MESH)
    pl.semaphore_wait(barrier, 7)

    def columns(zz, group):
        return pl.ds(pl.multiple_of((zz * near + group) * size, size), size)

    def spot(zz, r, source):
        return whole.at[zz * near + r, pl.ds(source * samples, samples)]

    def item(mask, k):
        kind, zz, r = ITEMS[mask][k]
        if kind == "own":
            source = library_ref.at[:, columns(zz, flip(place, r ^ mask))]
            target = spot(zz, r, mask)
        else:
            source = spot(zz, r ^ mask, 3 ^ mask)
            target = spot(zz, r, 3)
        return remote(source, target, plane_send.at[mask - 1, k], plane_recv.at[mask - 1, k], chip(mask))

    seen, sent = set(), []

    def arrive(mask, k):
        if (mask, k) not in seen:
            seen.add((mask, k))
            item(mask, k).wait_recv()

    def send(mask, k):
        kind, zz, r = ITEMS[mask][k]
        if kind == "fwd":
            arrive(3 ^ mask, ITEMS[3 ^ mask].index(("own", zz, r ^ mask)))
        item(mask, k).start()
        sent.append((mask, k))

    def both(action, k):
        action(1, k)
        action(2, k)

    copies = []
    for zz in range(2):
        for r in range(4):
            copies.append(pltpu.make_async_copy(
                library_ref.at[:, columns(zz, flip(place, r))], spot(zz, r, 0), own_sem.at[zz * near + r]))
    head_copy = pltpu.make_async_copy(library_ref.at[:, 0:128], head_raw, own_sem.at[8])
    head_copy.start()
    copies[0].start()
    copies[near].start()
    for k in range(3):
        both(send, k)
    for index, copy in enumerate(copies):
        if index % near:
            copy.start()

    placed = set()

    def landed_own(zz, r):
        if (zz, r) not in placed:
            placed.add((zz, r))
            copies[zz * near + r].wait()

    def head_over():
        return remote(heads, heads, head_send.at[0], head_recv.at[0], other)

    head_copy.wait()

    @pl.when(core == 0)
    def _():
        heads[...] = head_raw[...].T[0:width, :]
        head_over().start()

    def piece(zz, source, half):
        target = left.at[2 * half + zz, :, pl.ds(source * samples, samples)]
        index = zz * near + source
        return remote(target, target, left_send.at[index], left_recv.at[index], other)

    def turn(zz, source):
        left[2 * core + zz, :, source * samples:(source + 1) * samples] = (
            whole[zz * near, source * samples:(source + 1) * samples, :].T
        )
        piece(zz, source, core).start()

    for zz in range(2):
        landed_own(zz, 0)
        turn(zz, 0)
    for zz, r in STEPS:
        landed_own(zz, r)

    @pl.when(core == 1)
    def _():
        head_over().wait_recv()

    def first_far(step):
        peer = beside(step)
        return remote(first_part.at[peer], first_landed.at[step], first_send.at[0, step], first_recv.at[0, step],
                      floor(peer))

    def first_close(mask):
        return remote(first_sum.at[mask], first_near.at[mask], first_send.at[1, mask], first_recv.at[1, mask],
                      chip(mask))

    for zz in range(2):
        for r in range(near):
            value = jnp.dot(heads[...], whole[zz * near + r, 0:samples, :], preferred_element_type=full)
            first_part[2 * zz, r] = value[:, 0:chunk]
            first_part[2 * zz + 1, r] = value[:, chunk:size]
    for step in (2, 1, 3):
        first_far(step).start()

    def squares(index, peak):
        value = whole[index, 0:samples, :].astype(full)
        return jnp.maximum(peak, jnp.sum(value * value, axis=0, keepdims=True))

    def keep(index, value):
        bounds[index] = jnp.broadcast_to(value, (8, 128))

    def bound(index):
        if index == 0:
            source, target, place_of = 0, 1, other
        elif index < near:
            source, target, place_of = 2, 2 + index, chip(index)
        else:
            source, target, place_of = 6, 6 + index - 3, floor(beside(index - 3))
        return remote(bounds.at[source], bounds.at[target], bound_send.at[index], bound_recv.at[index], place_of)

    def unit_of(which):
        slot = 6 + lax.rem(level - which + far, far)
        return bounds[slot][0:1, 0:1]

    keep(0, jnp.max(
        lax.fori_loop(0, 2 * near, squares, jnp.zeros((1, size), full)), axis=1, keepdims=True))
    bound(0).start()
    both(arrive, 0)
    turn(0, 1)
    turn(0, 2)
    bound(0).wait_recv()
    keep(2, jnp.maximum(bounds[0], bounds[1])[0:1, 0:1])
    for mask in (3, 1, 2):
        bound(mask).start()
    both(arrive, 1)
    both(send, 3)
    both(arrive, 2)
    value = first_part[level]
    for step in range(1, far):
        first_far(step).wait_recv()
        value = value + first_landed[step]
    first_sum[...] = value
    for mask in (3, 1, 2):
        first_close(mask).start()
    both(send, 4)
    for mask in (1, 2, 3):
        bound(mask).wait_recv()
    keep(6, jnp.maximum(bounds[2] + bounds[3] + bounds[4] + bounds[5], 1e-30)[0:1, 0:1])
    for step in (2, 1, 3):
        bound(3 + step).start()
    turn(1, 1)
    turn(1, 2)

    both(arrive, 3)
    both(send, 5)
    turn(0, 3)
    turn(1, 3)
    for step in range(1, far):
        bound(3 + step).wait_recv()
    unit_own = unit_of(level)
    unit_pair = unit_own + unit_of(buddy)
    unit_buddy = unit_of(buddy)
    unit_far = unit_of(base) + unit_of(base + 1)

    def scatter(which, step):
        peer = beside(step)
        return remote(part.at[which, peer], landed.at[which, step], sum_send.at[which, 0, step],
                      sum_recv.at[which, 0, step], floor(peer))

    def spread(which, step, arriving=False):
        spot_of = summed.at[which, beside(far - step)] if arriving else summed.at[which, level]
        return remote(spot_of, spot_of, sum_send.at[which, 1, step], sum_recv.at[which, 1, step], floor(beside(step)))

    def fan(which, mask):
        return remote(summed.at[which], gathered.at[which, mask], sum_send.at[which, 2, mask],
                      sum_recv.at[which, 2, mask], chip(mask))

    def begin_sum(which):
        for step in (2, 1, 3):
            scatter(which, step).start()

    def add_up(which):
        value = part[which, level]
        for step in range(1, far):
            scatter(which, step).wait_recv()
            value = value + landed[which, step]
        summed[which, level] = value
        for step in (2, 1, 3):
            spread(which, step).start()

    def fan_out(which):
        for step in range(1, far):
            spread(which, step, True).wait_recv()
        for mask in (3, 1, 2):
            fan(which, mask).start()
        gathered[which, 0] = summed[which]

    def fan_in(which):
        for mask in range(1, near):
            fan(which, mask).wait_recv()

    def end_sum(which):
        for step in range(1, far):
            if which:
                scatter(which, step).wait_send()
            else:
                first_far(step).wait_send()
            spread(which, step).wait_send()
        for mask in range(1, near):
            fan(which, mask).wait_send()

    value = first_sum[0]
    for mask in range(1, near):
        first_close(mask).wait_recv()
        value = value + first_near[mask]
    summed[0, level] = value
    for step in (2, 1, 3):
        spread(0, step).start()

    def share(t, kind, which=0):
        if kind == "a":
            return remote(code_a.at[t], land_a.at[t], z_send.at[t, 0], z_recv.at[t, 0], floor(buddy))
        if kind == "c":
            return remote(code_c.at[t, which], land_c.at[t, which], z_send.at[t, 1 + which],
                          z_recv.at[t, 1 + which], floor(buddy))
        return remote(code_c.at[t, which], land_b.at[t], z_send.at[t, 1 + which], z_recv.at[t, 3],
                      floor(base + which))

    def combine(t):
        @pl.when(inner)
        def _():
            def one(which, carry):
                share(t, "c", which).wait_recv()
                encode(prod[t, base + which] + decode(land_c.at[t, which], unit_buddy), code_c.at[t, which], unit_pair)
                share(t, "b", which).start()
                return carry

            lax.fori_loop(0, 2, one, 0)

    def multiply(t):
        zz, r = STEPS[t]
        for k in range(READY[t]):
            both(arrive, k)
        landed_own(zz, r)

        def product(target):
            prod[t, target] = jnp.dot(left[target], whole[zz * near + r], preferred_element_type=full)

        def one(which, carry):
            product(base + which)

            @pl.when(outer)
            def _():
                encode(prod[t, base + which], code_c.at[t, which], unit_own)
                share(t, "c", which).start()

            return carry

        lax.fori_loop(0, 2, one, 0)
        product(buddy)
        encode(prod[t, buddy], code_a.at[t], unit_own)
        product(level)

    def send_a(t):
        share(t, "a").start()

    for zz in range(2):
        for source in range(4):
            piece(zz, source, 1 - core).wait_recv()
    multiply(0)
    multiply(1)
    fan_out(0)
    both(send, 6)
    send_a(0)
    send_a(1)
    combine(0)
    fan_in(0)

    def over(which):
        if which == 0:
            return remote(gathered.at[0], crossed, core_send.at[0], core_recv.at[0], other)
        return remote(sample_dots.at[0], sample_dots.at[1], core_send.at[1], core_recv.at[1], other)

    over(0).start()
    multiply(2)
    multiply(3)
    over(0).wait_recv()

    first = jnp.broadcast_to(scale_ref[:, 0:128], (8, 128)).T[0:width, 0:1] * (1.0 / total)
    for mask in range(near):
        for k in range(4):
            column = ((k // 2) * near + flip(place, mask)) * size + (k % 2) * chunk
            for side, half in ((0, core), (1, 1 - core)):
                cols = pl.ds(pl.multiple_of(half * block + column, chunk), chunk)
                value = gathered[0, mask, k] if side == 0 else crossed[mask, k]
                work[:, cols] = value * (first * scale_ref[:, cols])

    for group in range(width // 8):
        reflect_group(8 * group, work, vectors, taus, inner_dots)
        if group == 0:
            both(send, 7)
            combine(1)
        if group == 1:
            send_a(2)
            send_a(3)
        if group == 2:
            both(send, 8)
            both(send, 9)
        if group == 3:
            combine(2)
        if group == 4:
            both(send, 10)
        if group == 5:
            combine(3)

    def dots(zz, r):
        cols = columns(zz, flip(place, r))
        there = pl.ds(pl.multiple_of(core * block + (zz * near + flip(place, r)) * size, size), size)
        value = vectors[:, there] * scale_ref[:, there]
        high, low = halves_of(value)
        thin[zz * near + r] = jnp.concatenate([high, low], axis=0).T

    for zz in range(2):
        for r in range(4):
            dots(zz, r)
    value = jnp.dot(whole[0, 0:samples, :], thin[0], preferred_element_type=full)
    for index in range(1, 2 * near):
        value = value + jnp.dot(whole[index, 0:samples, :], thin[index], preferred_element_type=full)
    value = value.T
    sample_dots[0] = value[0:width, :] + value[width:2 * width, :]
    over(1).start()
    multiply(4)
    triangle(vectors, taus, factor)
    over(1).wait_recv()
    value = lax.dot_general(
        factor[...], sample_dots[0] + sample_dots[1], (((0,), (0,)), ((), ())), precision=HIGH,
        preferred_element_type=full)
    high, low = halves_of(value)
    stacked[0:width, 0:samples] = high
    stacked[width:2 * width, 0:samples] = low

    def stack(mask):
        return remote(stacked.at[:, 0:samples], stacked.at[:, mask * samples:(mask + 1) * samples],
                      sum_send.at[2, 2, mask], sum_recv.at[2, 2, mask], chip(mask))

    for mask in (3, 1, 2):
        stack(mask).start()
    both(send, 11)
    multiply(5)
    combine(4)
    for mask in (1, 2, 3):
        stack(mask).wait_recv()
    for zz in range(2):
        value = jnp.dot(stacked[...], whole[zz * near], preferred_element_type=full)
        value = value[0:width, :] + value[width:2 * width, :]
        part[1, 2 * zz] = value[:, 0:chunk]
        part[1, 2 * zz + 1] = value[:, chunk:size]
    begin_sum(1)
    send_a(4)
    combine(5)
    add_up(1)
    multiply(6)
    fan_out(1)
    multiply(7)
    send_a(5)
    send_a(6)
    send_a(7)
    combine(6)

    mine = pl.ds(pl.multiple_of(me * size, size), size)
    ours = vectors[:, mine]
    own_ref[...] = ours
    high, low = halves_of(ours)
    thin_rows = jnp.concatenate([high, high, low, low], axis=0).T
    row_scale = jnp.broadcast_to(scale_ref[:, mine], (8, size)).T[:, 0:1] * (1.0 / total)
    combine(7)
    fan_in(1)

    for t, (zz, r) in enumerate(STEPS):
        cols = columns(zz, flip(place, r))
        there = pl.ds(pl.multiple_of(core * block + (zz * near + flip(place, r)) * size, size), size)
        scale = scale_ref[:, there]
        value = jnp.concatenate([gathered[1, r, 2 * zz], gathered[1, r, 2 * zz + 1]], axis=1)
        high, low = halves_of(value * (scale * (1.0 / total)))
        change = jnp.dot(thin_rows, jnp.concatenate([high, low, high, low], axis=0), preferred_element_type=full)
        share(t, "a").wait_recv()
        share(t, "b").wait_recv()
        value = prod[t, level] + decode(land_a.at[t], unit_buddy) + decode(land_b.at[t], unit_far)
        updated_ref[:, cols] = value * (row_scale * scale) - change

    for mask, k in sent:
        item(mask, k).wait_send()
    for zz in range(2):
        for source in range(4):
            piece(zz, source, core).wait_send()
    for t in range(len(STEPS)):
        share(t, "a").wait_send()
        for which in range(2):
            share(t, "c", which).wait_send()
    end_sum(0)
    end_sum(1)
    for mask in range(1, near):
        stack(mask).wait_send()
    for index in range(7):
        bound(index).wait_send()
    over(0).wait_send()
    over(1).wait_send()

    for mask in range(1, near):
        first_close(mask).wait_send()

    @pl.when(core == 0)
    def _():
        head_over().wait_send()


def whole_update(library, col_scale, far):
    samples, block = library.shape
    near, cores = 4, 2
    columns = block * cores
    size = columns // (near * far)
    steps = block // size
    half, full = jnp.bfloat16, jnp.float32
    coded = (size, size)
    dma = pltpu.SemaphoreType.DMA
    vmem = pl.BlockSpec(memory_space=pltpu.VMEM)
    small = (PANEL, size // 2)
    updated, own = pl.pallas_call(
        functools.partial(whole_kernel, samples * near * far),
        out_shape=(jax.ShapeDtypeStruct((size, block), full), jax.ShapeDtypeStruct((PANEL, size), full)),
        in_specs=[pl.BlockSpec(memory_space=pl.ANY), vmem],
        out_specs=(vmem, vmem),
        scratch_shapes=[
            pltpu.VMEM((steps, near * samples, size), half), pltpu.VMEM((far, size, near * samples), half),
            pltpu.VMEM((steps, far, size, size), full),
            pltpu.VMEM((steps,) + coded, half), pltpu.VMEM((steps, 2) + coded, half),
            pltpu.VMEM((steps,) + coded, half), pltpu.VMEM((steps,) + coded, half),
            pltpu.VMEM((steps, 2) + coded, half),
            pltpu.VMEM((samples, 128), half), pltpu.VMEM((PANEL, samples), half),
            pltpu.VMEM((2, far) + small, full), pltpu.VMEM((2, far) + small, full),
            pltpu.VMEM((2, far) + small, full), pltpu.VMEM((2, near, far) + small, full),
            pltpu.VMEM((near, far) + small, full),
            pltpu.VMEM((PANEL, columns), full), pltpu.VMEM((PANEL, columns), full),
            pltpu.VMEM((PANEL, 128), full), pltpu.VMEM((8, 8, 128), full), pltpu.VMEM((PANEL, PANEL), full),
            pltpu.VMEM((2, PANEL, samples), full), pltpu.VMEM((2 * PANEL, near * samples), half),
            pltpu.VMEM((steps, size, 2 * PANEL), half), pltpu.VMEM((10, 8, 128), full),
            pltpu.VMEM((far, near) + small, full), pltpu.VMEM((far, near) + small, full),
            pltpu.VMEM((near,) + small, full), pltpu.VMEM((near,) + small, full),
            dma((2, 12)), dma((2, 12)), dma((9,)), dma((8,)), dma((8,)), dma((steps, 3)), dma((steps, 4)),
            dma((4,)), dma((4,)), dma((3, 3, 4)), dma((3, 3, 4)), dma((2,)), dma((2,)), dma((7,)), dma((7,)), dma((2, 4)), dma((2, 4)),
        ],
        compiler_params=pltpu.CompilerParams(
            vmem_limit_bytes=44 << 20, collective_id=1, has_side_effects=True
        ),
        cost_estimate=pl.CostEstimate(flops=12_000_000_000, bytes_accessed=10_000_000, transcendentals=0),
    )(library, col_scale)
    return updated, own.T


def per_device(library, col_scale):
    rows_dev, col_block = library.shape
    count_rows = lax.axis_size("rows")
    count_grid = lax.axis_size("grid")
    columns = col_block * count_grid
    row_block = columns // count_rows
    total = rows_dev * count_rows
    near = 1
    while near * near < count_rows:
        near *= 2
    far = count_rows // near
    if count_rows == 16 and count_grid == 2 and row_block % 256 == 0 and rows_dev % 128 == 0:
        return whole_update(library, col_scale[None, :], 4)
    grid_place = lax.axis_index("grid")
    rows_place = lax.axis_index("rows")
    near_groups = [[f * near + n for n in range(near)] for f in range(far)]
    far_groups = [[f * near + n for f in range(far)] for n in range(near)]
    own_scale = lax.dynamic_slice_in_dim(col_scale, grid_place * col_block, col_block)

    head = lax.all_gather(library[:, :PANEL], "grid", axis=0)[0]
    panel_part = lax.dot_general(
        head, library, (((0,), (0,)), ((), ())), preferred_element_type=jnp.float32
    )
    panel_part = panel_part * (col_scale[:PANEL, None] * own_scale[None, :] / total)
    vectors, mixed = panel_chain(panel_part, library, own_scale[None, :], count_rows, count_grid)
    mixed = mixed / total

    whole = lax.all_gather(library, "rows", axis=0, tiled=True, axis_index_groups=near_groups)
    whole, vectors, mixed = lax.optimization_barrier((whole, vectors, mixed))
    place = rows_place % near
    blocks = whole.T.reshape(far // count_grid, near, row_block, near * rows_dev)
    left = lax.dynamic_index_in_dim(blocks, place, 1, keepdims=False)
    left = left.reshape(far // count_grid * row_block, near * rows_dev)
    left = lax.all_gather(left, "grid", axis=0, tiled=True)
    product = lax.dot_general(
        left, whole, (((1,), (0,)), ((), ())), preferred_element_type=jnp.float32
    )
    gram = lax.psum_scatter(
        product, "rows", scatter_dimension=0, tiled=True, axis_index_groups=far_groups
    )
    row_scale = lax.dynamic_slice_in_dim(col_scale, rows_place * row_block, row_block)

    own_vectors = lax.dynamic_slice_in_dim(vectors, rows_place * row_block, row_block, 1).T
    gram = gram * (row_scale[:, None] * own_scale[None, :] / total)
    updated = gram - jnp.dot(own_vectors, mixed, precision=HIGH)
    return (updated, own_vectors)


def solution(mesh):
    return jax.shard_map(
        per_device,
        mesh=mesh,
        in_specs=(P("rows", "grid"), P()),
        out_specs=(P("rows", "grid"), P("rows", None)),
        check_vma=False,
    )
```

```python
import functools

import jax
import jax.numpy as jnp
from jax import lax
from jax.experimental import pallas as pl
from jax.experimental.pallas import tpu as pltpu
from jax.sharding import PartitionSpec as P

PANEL = 64
HIGH = lax.Precision.HIGHEST
MESH = pl.DeviceIdType.MESH


def reflect(vectors_ref, weights_ref, work, inner, taus):
    width, size = work.shape
    lane = lax.broadcasted_iota(jnp.int32, (1, size), 1)
    for base in range(0, width, 8):

        def one_step(step, carry, base=base):
            place = base + step
            row = work[pl.ds(place, 1), :]
            row = jnp.where(lane >= place, row, 0.0)
            pivot = jnp.sum(jnp.where(lane == place, row, 0.0), axis=1, keepdims=True)
            length = jnp.sqrt(jnp.sum(row * row, axis=1, keepdims=True))
            signed = jnp.where(pivot >= 0.0, length, -length)
            vector = row + jnp.where(lane == place, signed, 0.0)
            tau = 1.0 / (length * (length + jnp.abs(pivot)))
            rest = work[base:, :]
            project = jnp.sum(rest * vector, axis=1, keepdims=True)
            work[base:, :] = rest - (tau * project) * vector
            vectors_ref[pl.ds(place, 1), :] = vector
            taus[pl.ds(place, 1), :] = jnp.broadcast_to(tau, (1, 128))
            return carry

        lax.fori_loop(0, 8, one_step, 0)
    vectors = vectors_ref[...]
    inner[...] = lax.dot_general(
        vectors, vectors, (((1,), (1,)), ((), ())), precision=HIGH, preferred_element_type=jnp.float32
    )
    across = lax.broadcasted_iota(jnp.int32, (width, width), 1)
    down = lax.broadcasted_iota(jnp.int32, (width, 1), 0)

    def factor_step(place, factor):
        tau = taus[pl.ds(place, 1), 0:1]
        coupling = jnp.where(across < place, inner[pl.ds(place, 1), :] * factor, 0.0)
        column = -tau * jnp.sum(coupling, axis=1, keepdims=True)
        column = column + jnp.where(down == place, tau, 0.0)
        return jnp.where(across == place, column, factor)

    factor = lax.fori_loop(0, width, factor_step, jnp.zeros((width, width), jnp.float32))
    weights_ref[...] = lax.dot_general(
        factor, vectors, (((0,), (0,)), ((), ())), precision=HIGH, preferred_element_type=jnp.float32
    )


def remote(source, target, send, recv, place):
    return pltpu.make_async_remote_copy(
        src_ref=source, dst_ref=target, send_sem=send, recv_sem=recv,
        device_id=place, device_id_type=pl.DeviceIdType.MESH,
    )


def sum_rows(count, part, landed, out, sems):
    me, core = lax.axis_index("rows"), lax.axis_index("grid")
    send, recv, send_back, recv_back = sems

    def scatter(step):
        peer = lax.rem(me + step, count)
        return remote(part.at[peer], landed.at[step], send.at[step], recv.at[step], (peer, core))

    def spread(step):
        peer = lax.rem(me + step, count)
        return remote(out.at[me], out.at[me], send_back.at[step], recv_back.at[step], (peer, core))

    def arrival(step):
        peer = lax.rem(me + count - step, count)
        return remote(out.at[peer], out.at[peer], send_back.at[step], recv_back.at[step], (peer, core))

    def loop(action):
        def body(step, carry):
            action(step)
            return carry
        lax.fori_loop(1, count, body, 0)

    loop(lambda step: scatter(step).start())
    loop(lambda step: scatter(step).wait_recv())
    total = part[me]
    for step in range(1, count):
        total = total + landed[step]
    out[me] = total
    loop(lambda step: spread(step).start())
    loop(lambda step: arrival(step).wait_recv())
    loop(lambda step: scatter(step).wait_send())
    loop(lambda step: spread(step).wait_send())


def panel_kernel(
    count, cores, part_ref, library_ref, scale_ref, vectors_ref, mixed_ref,
    part, landed, gathered, part_two, landed_two, gathered_two, halves,
    weights, work, inner, taus, row_sems, row_sems_two, core_sems, half_sems,
):
    me, core = lax.axis_index("rows"), lax.axis_index("grid")
    width, block = part_ref.shape
    per = width // count
    barrier = pltpu.get_barrier_semaphore()

    def greet(step, carry):
        pl.semaphore_signal(
            barrier, inc=1, device_id=(lax.rem(me + step, count), core), device_id_type=pl.DeviceIdType.MESH
        )
        return carry

    lax.fori_loop(1, count, greet, 0)
    for step in range(1, cores):
        pl.semaphore_signal(
            barrier, inc=1, device_id=(me, lax.rem(core + step, cores)), device_id_type=pl.DeviceIdType.MESH
        )
    for place in range(count):
        part[place] = part_ref[place * per:(place + 1) * per, :]
    pl.semaphore_wait(barrier, count + cores - 2)

    sum_rows(count, part, landed, gathered.at[core], [row_sems.at[k] for k in range(4)])
    shares = []
    for step in range(1, cores):
        peer = lax.rem(core + step, cores)
        shares.append(
            remote(gathered.at[core], gathered.at[core], core_sems.at[0, step], core_sems.at[1, step], (me, peer))
        )
        shares[-1].start()
    for step in range(1, cores):
        peer = lax.rem(core + cores - step, cores)
        remote(
            gathered.at[peer], gathered.at[peer], core_sems.at[0, step], core_sems.at[1, step], (me, peer)
        ).wait_recv()
    for share in shares:
        share.wait_send()
    for half in range(cores):
        for place in range(count):
            work[place * per:(place + 1) * per, half * block:(half + 1) * block] = gathered[half, place]

    reflect(vectors_ref, weights, work, inner, taus)

    step_cols = min(block, 512)
    halves[0] = jnp.zeros_like(halves[0])
    for start in range(0, block, step_cols):
        cols = slice(start, start + step_cols)
        own = weights[:, pl.ds(pl.multiple_of(core * block + start, 128), step_cols)] * scale_ref[:, cols]
        halves[0] += lax.dot_general(
            own, library_ref[:, cols].astype(jnp.float32), (((1,), (1,)), ((), ())),
            precision=HIGH, preferred_element_type=jnp.float32,
        )
    shares = []
    for step in range(1, cores):
        peer = lax.rem(core + step, cores)
        shares.append(
            remote(halves.at[0], halves.at[step], half_sems.at[0, step], half_sems.at[1, step], (me, peer))
        )
        shares[-1].start()
    for share in shares:
        share.wait()
    summed = halves[0]
    for step in range(1, cores):
        summed = summed + halves[step]
    for start in range(0, block, step_cols):
        cols = slice(start, start + step_cols)
        chunk = jnp.dot(
            summed, library_ref[:, cols].astype(jnp.float32), precision=HIGH, preferred_element_type=jnp.float32
        )
        for place in range(count):
            part_two[place, :, cols] = chunk[place * per:(place + 1) * per, :]
    sum_rows(count, part_two, landed_two, gathered_two, [row_sems_two.at[k] for k in range(4)])
    for place in range(count):
        mixed_ref[place * per:(place + 1) * per, :] = gathered_two[place] * scale_ref[...]


def panel_chain(part, library, scale, count, cores):
    width, block = part.shape
    rows_dev = library.shape[0]
    per = width // count
    size = block * cores
    real = jnp.float32
    slices = pltpu.VMEM((count, per, block), real)
    return pl.pallas_call(
        functools.partial(panel_kernel, count, cores),
        out_shape=(jax.ShapeDtypeStruct((width, size), real), jax.ShapeDtypeStruct((width, block), real)),
        in_specs=[pl.BlockSpec(memory_space=pltpu.VMEM)] * 3,
        out_specs=(pl.BlockSpec(memory_space=pltpu.VMEM),) * 2,
        scratch_shapes=[
            slices, slices, pltpu.VMEM((cores, count, per, block), real),
            slices, slices, slices, pltpu.VMEM((cores, width, rows_dev), real),
            pltpu.VMEM((width, size), real), pltpu.VMEM((width, size), real),
            pltpu.VMEM((width, width), real), pltpu.VMEM((width, 128), real),
            pltpu.SemaphoreType.DMA((4, count)), pltpu.SemaphoreType.DMA((4, count)),
            pltpu.SemaphoreType.DMA((2, cores)), pltpu.SemaphoreType.DMA((2, cores)),
        ],
        compiler_params=pltpu.CompilerParams(
            vmem_limit_bytes=32 << 20, collective_id=0, has_side_effects=True
        ),
        cost_estimate=pl.CostEstimate(flops=20_000_000_000, bytes_accessed=200_000_000, transcendentals=0),
    )(part, library, scale)


X_ITEMS = (
    ("own", 0, 0), ("own", 1, 2), ("own", 1, 0), ("fwd", 0, 0), ("own", 0, 1), ("fwd", 0, 1),
    ("own", 1, 3), ("own", 1, 1), ("fwd", 0, 2), ("own", 0, 2), ("fwd", 0, 3), ("own", 0, 3),
)
Y_ITEMS = (
    ("own", 0, 0), ("own", 0, 1), ("own", 1, 0), ("fwd", 1, 0), ("own", 1, 2), ("fwd", 1, 2),
    ("own", 0, 3), ("own", 0, 2), ("fwd", 1, 1), ("own", 1, 1), ("fwd", 1, 3), ("own", 1, 3),
)
ITEMS = {1: X_ITEMS, 2: Y_ITEMS}
STEPS = ((0, 0), (1, 0), (0, 1), (1, 2), (0, 2), (1, 1), (0, 3), (1, 3))
READY = (4, 4, 6, 6, 10, 10, 12, 12)
TOP = 2.0 ** 15.5
LEAST = 2.0 ** -125


def flip(place, mask):
    low, high = lax.rem(place, 2), place // 2
    low = 1 - low if mask & 1 else low
    high = 1 - high if mask & 2 else high
    return high * 2 + low


def encode(value, target, unit):
    level = value * (TOP / unit)
    square = level * level
    fourth = square * square
    eighth = fourth * fourth
    target[...] = jnp.where(level < 0.0, -eighth, eighth).astype(jnp.bfloat16)


def decode(source, unit):
    code = source[...].astype(jnp.float32)
    second = lax.rsqrt(lax.rsqrt(jnp.maximum(jnp.abs(code), LEAST)))
    value = second * lax.rsqrt(second) * (unit * (1.0 / TOP))
    return jnp.where(code < 0.0, -value, value)


def reflect_group(base, work, vectors, taus, inner):
    width, size = work.shape
    lane = lax.broadcasted_iota(jnp.int32, (1, 128), 1)

    def one_step(step, carry):
        place = base + step
        row = work[pl.ds(place, 1), :]
        head, tail = jnp.where(lane >= place, row[:, 0:128], 0.0), row[:, 128:size]
        near = work[base:base + 8, 0:128]
        rest = work[base:base + 8, 128:size]
        square = jnp.sum(head * head, axis=1, keepdims=True) + jnp.sum(tail * tail, axis=1, keepdims=True)
        pivot = jnp.sum(jnp.where(lane == place, head, 0.0), axis=1, keepdims=True)
        project = jnp.sum(near * head, axis=1, keepdims=True) + jnp.sum(rest * tail, axis=1, keepdims=True)
        across = jnp.sum(jnp.where(lane == place, near, 0.0), axis=1, keepdims=True)
        length = jnp.sqrt(square)
        signed = jnp.where(pivot >= 0.0, length, -length)
        tau = 1.0 / (length * (length + jnp.abs(pivot)))
        weight = tau * (project + signed * across)
        head = head + jnp.where(lane == place, signed, 0.0)
        work[base:base + 8, 0:128] = near - weight * head
        work[base:base + 8, 128:size] = rest - weight * tail
        vectors[pl.ds(place, 1), :] = jnp.concatenate([head, tail], axis=1)
        taus[pl.ds(place, 1), :] = jnp.broadcast_to(tau, (1, 128))
        return carry

    lax.fori_loop(0, 8, one_step, 0)
    if base + 8 == width:
        return

    def couple(step, carry):
        column = jnp.sum(vectors[base:base + 8, :] * vectors[pl.ds(base + step, 1), :], axis=1, keepdims=True)
        inner[step] = jnp.broadcast_to(column, (8, 128))
        return carry

    lax.fori_loop(0, 8, couple, 0, unroll=True)

    def trail(group, carry):
        rows = pl.ds(pl.multiple_of(group * 8, 8), 8)
        rest = work[rows, :]
        dots = [jnp.sum(rest * vectors[base + k:base + k + 1, :], axis=1, keepdims=True) for k in range(8)]
        weights = []
        for k in range(8):
            value = dots[k]
            for i in range(k):
                value = value - weights[i] * inner[k, i:i + 1, :]
            weights.append(value * taus[base + k:base + k + 1, :])
        for k in range(8):
            rest = rest - weights[k][:, 0:1] * vectors[base + k:base + k + 1, :]
        work[rows, :] = rest
        return carry

    lax.fori_loop(base // 8 + 1, width // 8, trail, 0, unroll=True)


def triangle(vectors, taus, factor_ref):
    width = vectors.shape[0]
    rows = vectors[...]
    gram = lax.dot_general(rows, rows, (((1,), (1,)), ((), ())), precision=HIGH, preferred_element_type=jnp.float32)
    across = lax.broadcasted_iota(jnp.int32, (width, width), 1)
    down = lax.broadcasted_iota(jnp.int32, (width, width), 0)
    factor = jnp.where(across == down, taus[:, 0:1], 0.0)
    span = 1
    while span < width:
        pick = (down // span + 1 == across // span) & (across // (2 * span) == down // (2 * span))
        middle = jnp.dot(factor, jnp.where(pick, gram, 0.0), precision=HIGH, preferred_element_type=jnp.float32)
        factor = factor - jnp.dot(middle, factor, precision=HIGH, preferred_element_type=jnp.float32)
        span *= 2
    factor_ref[...] = factor


def halves_of(value):
    high = value.astype(jnp.bfloat16)
    return high, (value - high.astype(jnp.float32)).astype(jnp.bfloat16)


def whole_kernel(
    total, library_ref, scale_ref, updated_ref, own_ref,
    whole, left, prod, code_a, code_c, land_a, land_b, land_c,
    head_raw, heads, part, landed, summed, gathered, crossed, work, vectors, taus, inner_dots, factor,
    sample_dots, stacked, thin, bounds, first_part, first_landed, first_sum, first_near,
    plane_send, plane_recv, own_sem, left_send, left_recv, z_send, z_recv,
    head_send, head_recv, sum_send, sum_recv, core_send, core_recv, bound_send, bound_recv, first_send, first_recv,
):
    me, core = lax.axis_index("rows"), lax.axis_index("grid")
    far, near = left.shape[0], 4
    place, level = lax.rem(me, near), me // near
    samples = library_ref.shape[0]
    size = left.shape[1]
    block = library_ref.shape[1]
    width = work.shape[0]
    chunk = size // 2
    buddy = level + 1 - 2 * lax.rem(level, 2)
    base = 2 * (1 - level // 2)
    inner = lax.rem(level + 1, far) // 2 == 1
    outer = lax.rem(level + 1, far) // 2 == 0
    other = (me, 1 - core)
    full = jnp.float32

    def chip(mask):
        return (level * near + flip(place, mask), core)

    def floor(which):
        return (which * near + place, core)

    def beside(step):
        return lax.rem(level + step, far)

    barrier = pltpu.get_barrier_semaphore()
    for target in (chip(1), chip(2), chip(3), floor(beside(1)), floor(beside(2)), floor(beside(3)), other):
        pl.semaphore_signal(barrier, inc=1, device_id=target, device_id_type=MESH)
    pl.semaphore_wait(barrier, 7)

    def columns(zz, group):
        return pl.ds(pl.multiple_of((zz * near + group) * size, size), size)

    def spot(zz, r, source):
        return whole.at[zz * near + r, pl.ds(source * samples, samples)]

    def item(mask, k):
        kind, zz, r = ITEMS[mask][k]
        if kind == "own":
            source = library_ref.at[:, columns(zz, flip(place, r ^ mask))]
            target = spot(zz, r, mask)
        else:
            source = spot(zz, r ^ mask, 3 ^ mask)
            target = spot(zz, r, 3)
        return remote(source, target, plane_send.at[mask - 1, k], plane_recv.at[mask - 1, k], chip(mask))

    seen, sent = set(), []

    def arrive(mask, k):
        if (mask, k) not in seen:
            seen.add((mask, k))
            item(mask, k).wait_recv()

    def send(mask, k):
        kind, zz, r = ITEMS[mask][k]
        if kind == "fwd":
            arrive(3 ^ mask, ITEMS[3 ^ mask].index(("own", zz, r ^ mask)))
        item(mask, k).start()
        sent.append((mask, k))

    def both(action, k):
        action(1, k)
        action(2, k)

    copies = []
    for zz in range(2):
        for r in range(4):
            copies.append(pltpu.make_async_copy(
                library_ref.at[:, columns(zz, flip(place, r))], spot(zz, r, 0), own_sem.at[zz * near + r]))
    head_copy = pltpu.make_async_copy(library_ref.at[:, 0:128], head_raw, own_sem.at[8])
    head_copy.start()
    copies[0].start()
    copies[near].start()
    for k in range(3):
        both(send, k)
    for index, copy in enumerate(copies):
        if index % near:
            copy.start()

    placed = set()

    def landed_own(zz, r):
        if (zz, r) not in placed:
            placed.add((zz, r))
            copies[zz * near + r].wait()

    def head_over():
        return remote(heads, heads, head_send.at[0], head_recv.at[0], other)

    head_copy.wait()

    @pl.when(core == 0)
    def _():
        heads[...] = head_raw[...].T[0:width, :]
        head_over().start()

    def piece(zz, source, half):
        target = left.at[2 * half + zz, :, pl.ds(source * samples, samples)]
        index = zz * near + source
        return remote(target, target, left_send.at[index], left_recv.at[index], other)

    def turn(zz, source):
        left[2 * core + zz, :, source * samples:(source + 1) * samples] = (
            whole[zz * near, source * samples:(source + 1) * samples, :].T
        )
        piece(zz, source, core).start()

    for zz in range(2):
        landed_own(zz, 0)
        turn(zz, 0)
    for zz, r in STEPS:
        landed_own(zz, r)

    @pl.when(core == 1)
    def _():
        head_over().wait_recv()

    def first_far(step):
        peer = beside(step)
        return remote(first_part.at[peer], first_landed.at[step], first_send.at[0, step], first_recv.at[0, step],
                      floor(peer))

    def first_close(mask):
        return remote(first_sum.at[mask], first_near.at[mask], first_send.at[1, mask], first_recv.at[1, mask],
                      chip(mask))

    for zz in range(2):
        for r in range(near):
            value = jnp.dot(heads[...], whole[zz * near + r, 0:samples, :], preferred_element_type=full)
            first_part[2 * zz, r] = value[:, 0:chunk]
            first_part[2 * zz + 1, r] = value[:, chunk:size]
    for step in (2, 1, 3):
        first_far(step).start()

    def squares(index, peak):
        value = whole[index, 0:samples, :].astype(full)
        return jnp.maximum(peak, jnp.sum(value * value, axis=0, keepdims=True))

    def keep(index, value):
        bounds[index] = jnp.broadcast_to(value, (8, 128))

    def bound(index):
        if index == 0:
            source, target, place_of = 0, 1, other
        elif index < near:
            source, target, place_of = 2, 2 + index, chip(index)
        else:
            source, target, place_of = 6, 6 + index - 3, floor(beside(index - 3))
        return remote(bounds.at[source], bounds.at[target], bound_send.at[index], bound_recv.at[index], place_of)

    def unit_of(which):
        slot = 6 + lax.rem(level - which + far, far)
        return bounds[slot][0:1, 0:1]

    keep(0, jnp.max(
        lax.fori_loop(0, 2 * near, squares, jnp.zeros((1, size), full)), axis=1, keepdims=True))
    bound(0).start()
    both(arrive, 0)
    turn(0, 1)
    turn(0, 2)
    bound(0).wait_recv()
    keep(2, jnp.maximum(bounds[0], bounds[1])[0:1, 0:1])
    for mask in (3, 1, 2):
        bound(mask).start()
    both(arrive, 1)
    both(send, 3)
    both(arrive, 2)
    value = first_part[level]
    for step in range(1, far):
        first_far(step).wait_recv()
        value = value + first_landed[step]
    first_sum[...] = value
    for mask in (3, 1, 2):
        first_close(mask).start()
    both(send, 4)
    for mask in (1, 2, 3):
        bound(mask).wait_recv()
    keep(6, jnp.maximum(bounds[2] + bounds[3] + bounds[4] + bounds[5], 1e-30)[0:1, 0:1])
    for step in (2, 1, 3):
        bound(3 + step).start()
    turn(1, 1)
    turn(1, 2)

    both(arrive, 3)
    both(send, 5)
    turn(0, 3)
    turn(1, 3)
    for step in range(1, far):
        bound(3 + step).wait_recv()
    unit_own = unit_of(level)
    unit_pair = unit_own + unit_of(buddy)
    unit_buddy = unit_of(buddy)
    unit_far = unit_of(base) + unit_of(base + 1)

    def scatter(which, step):
        peer = beside(step)
        return remote(part.at[which, peer], landed.at[which, step], sum_send.at[which, 0, step],
                      sum_recv.at[which, 0, step], floor(peer))

    def spread(which, step, arriving=False):
        spot_of = summed.at[which, beside(far - step)] if arriving else summed.at[which, level]
        return remote(spot_of, spot_of, sum_send.at[which, 1, step], sum_recv.at[which, 1, step], floor(beside(step)))

    def fan(which, mask):
        return remote(summed.at[which], gathered.at[which, mask], sum_send.at[which, 2, mask],
                      sum_recv.at[which, 2, mask], chip(mask))

    def begin_sum(which):
        for step in (2, 1, 3):
            scatter(which, step).start()

    def add_up(which):
        value = part[which, level]
        for step in range(1, far):
            scatter(which, step).wait_recv()
            value = value + landed[which, step]
        summed[which, level] = value
        for step in (2, 1, 3):
            spread(which, step).start()

    def fan_out(which):
        for step in range(1, far):
            spread(which, step, True).wait_recv()
        for mask in (3, 1, 2):
            fan(which, mask).start()
        gathered[which, 0] = summed[which]

    def fan_in(which):
        for mask in range(1, near):
            fan(which, mask).wait_recv()

    def end_sum(which):
        for step in range(1, far):
            if which:
                scatter(which, step).wait_send()
            else:
                first_far(step).wait_send()
            spread(which, step).wait_send()
        for mask in range(1, near):
            fan(which, mask).wait_send()

    value = first_sum[0]
    for mask in range(1, near):
        first_close(mask).wait_recv()
        value = value + first_near[mask]
    summed[0, level] = value
    for step in (2, 1, 3):
        spread(0, step).start()

    def share(t, kind, which=0):
        if kind == "a":
            return remote(code_a.at[t], land_a.at[t], z_send.at[t, 0], z_recv.at[t, 0], floor(buddy))
        if kind == "c":
            return remote(code_c.at[t, which], land_c.at[t, which], z_send.at[t, 1 + which],
                          z_recv.at[t, 1 + which], floor(buddy))
        return remote(code_c.at[t, which], land_b.at[t], z_send.at[t, 1 + which], z_recv.at[t, 3],
                      floor(base + which))

    def combine(t):
        @pl.when(inner)
        def _():
            def one(which, carry):
                share(t, "c", which).wait_recv()
                encode(prod[t, base + which] + decode(land_c.at[t, which], unit_buddy), code_c.at[t, which], unit_pair)
                share(t, "b", which).start()
                return carry

            lax.fori_loop(0, 2, one, 0)

    def multiply(t):
        zz, r = STEPS[t]
        for k in range(READY[t]):
            both(arrive, k)
        landed_own(zz, r)

        def product(target):
            prod[t, target] = jnp.dot(left[target], whole[zz * near + r], preferred_element_type=full)

        def one(which, carry):
            product(base + which)

            @pl.when(outer)
            def _():
                encode(prod[t, base + which], code_c.at[t, which], unit_own)
                share(t, "c", which).start()

            return carry

        lax.fori_loop(0, 2, one, 0)
        product(buddy)
        encode(prod[t, buddy], code_a.at[t], unit_own)
        product(level)

    def send_a(t):
        share(t, "a").start()

    for zz in range(2):
        for source in range(4):
            piece(zz, source, 1 - core).wait_recv()
    multiply(0)
    multiply(1)
    fan_out(0)
    both(send, 6)
    send_a(0)
    send_a(1)
    combine(0)
    fan_in(0)

    def over(which):
        if which == 0:
            return remote(gathered.at[0], crossed, core_send.at[0], core_recv.at[0], other)
        return remote(sample_dots.at[0], sample_dots.at[1], core_send.at[1], core_recv.at[1], other)

    over(0).start()
    multiply(2)
    multiply(3)
    over(0).wait_recv()

    first = jnp.broadcast_to(scale_ref[:, 0:128], (8, 128)).T[0:width, 0:1] * (1.0 / total)
    for mask in range(near):
        for k in range(4):
            column = ((k // 2) * near + flip(place, mask)) * size + (k % 2) * chunk
            for side, half in ((0, core), (1, 1 - core)):
                cols = pl.ds(pl.multiple_of(half * block + column, chunk), chunk)
                value = gathered[0, mask, k] if side == 0 else crossed[mask, k]
                work[:, cols] = value * (first * scale_ref[:, cols])

    for group in range(width // 8):
        reflect_group(8 * group, work, vectors, taus, inner_dots)
        if group == 0:
            both(send, 7)
            combine(1)
        if group == 1:
            send_a(2)
            send_a(3)
        if group == 2:
            both(send, 8)
            both(send, 9)
        if group == 3:
            combine(2)
        if group == 4:
            both(send, 10)
        if group == 5:
            combine(3)

    def dots(zz, r):
        cols = columns(zz, flip(place, r))
        there = pl.ds(pl.multiple_of(core * block + (zz * near + flip(place, r)) * size, size), size)
        value = vectors[:, there] * scale_ref[:, there]
        high, low = halves_of(value)
        thin[zz * near + r] = jnp.concatenate([high, low], axis=0).T

    for zz in range(2):
        for r in range(4):
            dots(zz, r)
    value = jnp.dot(whole[0, 0:samples, :], thin[0], preferred_element_type=full)
    for index in range(1, 2 * near):
        value = value + jnp.dot(whole[index, 0:samples, :], thin[index], preferred_element_type=full)
    value = value.T
    sample_dots[0] = value[0:width, :] + value[width:2 * width, :]
    over(1).start()
    multiply(4)
    triangle(vectors, taus, factor)
    over(1).wait_recv()
    value = lax.dot_general(
        factor[...], sample_dots[0] + sample_dots[1], (((0,), (0,)), ((), ())), precision=HIGH,
        preferred_element_type=full)
    high, low = halves_of(value)
    stacked[0:width, 0:samples] = high
    stacked[width:2 * width, 0:samples] = low

    def stack(mask):
        return remote(stacked.at[:, 0:samples], stacked.at[:, mask * samples:(mask + 1) * samples],
                      sum_send.at[2, 2, mask], sum_recv.at[2, 2, mask], chip(mask))

    for mask in (3, 1, 2):
        stack(mask).start()
    both(send, 11)
    multiply(5)
    for mask in (1, 2, 3):
        stack(mask).wait_recv()
    for zz in range(2):
        value = jnp.dot(stacked[...], whole[zz * near], preferred_element_type=full)
        value = value[0:width, :] + value[width:2 * width, :]
        part[1, 2 * zz] = value[:, 0:chunk]
        part[1, 2 * zz + 1] = value[:, chunk:size]
    begin_sum(1)
    send_a(4)
    combine(4)
    add_up(1)
    combine(5)
    multiply(6)
    fan_out(1)
    multiply(7)
    send_a(5)
    send_a(6)
    send_a(7)
    combine(6)

    mine = pl.ds(pl.multiple_of(me * size, size), size)
    ours = vectors[:, mine]
    own_ref[...] = ours
    high, low = halves_of(ours)
    thin_rows = jnp.concatenate([high, high, low, low], axis=0).T
    row_scale = jnp.broadcast_to(scale_ref[:, mine], (8, size)).T[:, 0:1] * (1.0 / total)
    combine(7)
    fan_in(1)

    for t, (zz, r) in enumerate(STEPS):
        cols = columns(zz, flip(place, r))
        there = pl.ds(pl.multiple_of(core * block + (zz * near + flip(place, r)) * size, size), size)
        scale = scale_ref[:, there]
        value = jnp.concatenate([gathered[1, r, 2 * zz], gathered[1, r, 2 * zz + 1]], axis=1)
        high, low = halves_of(value * (scale * (1.0 / total)))
        change = jnp.dot(thin_rows, jnp.concatenate([high, low, high, low], axis=0), preferred_element_type=full)
        share(t, "a").wait_recv()
        share(t, "b").wait_recv()
        value = prod[t, level] + decode(land_a.at[t], unit_buddy) + decode(land_b.at[t], unit_far)
        updated_ref[:, cols] = value * (row_scale * scale) - change

    for mask, k in sent:
        item(mask, k).wait_send()
    for zz in range(2):
        for source in range(4):
            piece(zz, source, core).wait_send()
    for t in range(len(STEPS)):
        share(t, "a").wait_send()
        for which in range(2):
            share(t, "c", which).wait_send()
    end_sum(0)
    end_sum(1)
    for mask in range(1, near):
        stack(mask).wait_send()
    for index in range(7):
        bound(index).wait_send()
    over(0).wait_send()
    over(1).wait_send()

    for mask in range(1, near):
        first_close(mask).wait_send()

    @pl.when(core == 0)
    def _():
        head_over().wait_send()


def whole_update(library, col_scale, far):
    samples, block = library.shape
    near, cores = 4, 2
    columns = block * cores
    size = columns // (near * far)
    steps = block // size
    half, full = jnp.bfloat16, jnp.float32
    coded = (size, size)
    dma = pltpu.SemaphoreType.DMA
    vmem = pl.BlockSpec(memory_space=pltpu.VMEM)
    small = (PANEL, size // 2)
    updated, own = pl.pallas_call(
        functools.partial(whole_kernel, samples * near * far),
        out_shape=(jax.ShapeDtypeStruct((size, block), full), jax.ShapeDtypeStruct((PANEL, size), full)),
        in_specs=[pl.BlockSpec(memory_space=pl.ANY), vmem],
        out_specs=(vmem, vmem),
        scratch_shapes=[
            pltpu.VMEM((steps, near * samples, size), half), pltpu.VMEM((far, size, near * samples), half),
            pltpu.VMEM((steps, far, size, size), full),
            pltpu.VMEM((steps,) + coded, half), pltpu.VMEM((steps, 2) + coded, half),
            pltpu.VMEM((steps,) + coded, half), pltpu.VMEM((steps,) + coded, half),
            pltpu.VMEM((steps, 2) + coded, half),
            pltpu.VMEM((samples, 128), half), pltpu.VMEM((PANEL, samples), half),
            pltpu.VMEM((2, far) + small, full), pltpu.VMEM((2, far) + small, full),
            pltpu.VMEM((2, far) + small, full), pltpu.VMEM((2, near, far) + small, full),
            pltpu.VMEM((near, far) + small, full),
            pltpu.VMEM((PANEL, columns), full), pltpu.VMEM((PANEL, columns), full),
            pltpu.VMEM((PANEL, 128), full), pltpu.VMEM((8, 8, 128), full), pltpu.VMEM((PANEL, PANEL), full),
            pltpu.VMEM((2, PANEL, samples), full), pltpu.VMEM((2 * PANEL, near * samples), half),
            pltpu.VMEM((steps, size, 2 * PANEL), half), pltpu.VMEM((10, 8, 128), full),
            pltpu.VMEM((far, near) + small, full), pltpu.VMEM((far, near) + small, full),
            pltpu.VMEM((near,) + small, full), pltpu.VMEM((near,) + small, full),
            dma((2, 12)), dma((2, 12)), dma((9,)), dma((8,)), dma((8,)), dma((steps, 3)), dma((steps, 4)),
            dma((4,)), dma((4,)), dma((3, 3, 4)), dma((3, 3, 4)), dma((2,)), dma((2,)), dma((7,)), dma((7,)), dma((2, 4)), dma((2, 4)),
        ],
        compiler_params=pltpu.CompilerParams(
            vmem_limit_bytes=44 << 20, collective_id=1, has_side_effects=True
        ),
        cost_estimate=pl.CostEstimate(flops=12_000_000_000, bytes_accessed=10_000_000, transcendentals=0),
    )(library, col_scale)
    return updated, own.T


def per_device(library, col_scale):
    rows_dev, col_block = library.shape
    count_rows = lax.axis_size("rows")
    count_grid = lax.axis_size("grid")
    columns = col_block * count_grid
    row_block = columns // count_rows
    total = rows_dev * count_rows
    near = 1
    while near * near < count_rows:
        near *= 2
    far = count_rows // near
    if count_rows == 16 and count_grid == 2 and row_block % 256 == 0 and rows_dev % 128 == 0:
        return whole_update(library, col_scale[None, :], 4)
    grid_place = lax.axis_index("grid")
    rows_place = lax.axis_index("rows")
    near_groups = [[f * near + n for n in range(near)] for f in range(far)]
    far_groups = [[f * near + n for f in range(far)] for n in range(near)]
    own_scale = lax.dynamic_slice_in_dim(col_scale, grid_place * col_block, col_block)

    head = lax.all_gather(library[:, :PANEL], "grid", axis=0)[0]
    panel_part = lax.dot_general(
        head, library, (((0,), (0,)), ((), ())), preferred_element_type=jnp.float32
    )
    panel_part = panel_part * (col_scale[:PANEL, None] * own_scale[None, :] / total)
    vectors, mixed = panel_chain(panel_part, library, own_scale[None, :], count_rows, count_grid)
    mixed = mixed / total

    whole = lax.all_gather(library, "rows", axis=0, tiled=True, axis_index_groups=near_groups)
    whole, vectors, mixed = lax.optimization_barrier((whole, vectors, mixed))
    place = rows_place % near
    blocks = whole.T.reshape(far // count_grid, near, row_block, near * rows_dev)
    left = lax.dynamic_index_in_dim(blocks, place, 1, keepdims=False)
    left = left.reshape(far // count_grid * row_block, near * rows_dev)
    left = lax.all_gather(left, "grid", axis=0, tiled=True)
    product = lax.dot_general(
        left, whole, (((1,), (0,)), ((), ())), preferred_element_type=jnp.float32
    )
    gram = lax.psum_scatter(
        product, "rows", scatter_dimension=0, tiled=True, axis_index_groups=far_groups
    )
    row_scale = lax.dynamic_slice_in_dim(col_scale, rows_place * row_block, row_block)

    own_vectors = lax.dynamic_slice_in_dim(vectors, rows_place * row_block, row_block, 1).T
    gram = gram * (row_scale[:, None] * own_scale[None, :] / total)
    updated = gram - jnp.dot(own_vectors, mixed, precision=HIGH)
    return (updated, own_vectors)


def solution(mesh):
    return jax.shard_map(
        per_device,
        mesh=mesh,
        in_specs=(P("rows", "grid"), P()),
        out_specs=(P("rows", "grid"), P("rows", None)),
        check_vma=False,
    )
```
